32 devices in a mesh: groups: 2 (over y), seq: 4 (over z), section: 2 (over x), mp: 2 (over core).
Axes of the slice: x: 2, y: 2, z: 4, core: 2. Of those that a mesh axis runs over, the one named last changes fastest.
Arguments:
- section_inputs: bfloat16 [2, 1024, 768], P('section', ('groups', 'seq')), parts along dimension 1, may hold values from -6 to 6
- cotangent: bfloat16 [1024, 768], P(('groups', 'seq')), parts along dimension 0, may hold values from -6 to 6
- w_in: bfloat16 [2, 768, 1536], P('section', None, 'mp'), may hold values from -0.21875 to 0.21875
- w_bc: bfloat16 [2, 768, 32], P('section'), may hold values from -0.21875 to 0.21875
- w_out: bfloat16 [2, 1536, 768], P('section', 'mp'), may hold values from -0.15625 to 0.15625
- decay_rates: float32 [2, 24], P('section', 'mp'), may hold values from 0.0001953125 to 0.05
- resets: int32 [1024], P(('groups', 'seq')), parts along dimension 0, may hold values 0 or 1
Outputs:
- grad_inputs: bfloat16 [2, 1024, 768], P('section', ('groups', 'seq')), parts along dimension 1
- grad_w_bc: float32 [2, 1536, 32], P('section', 'groups'), parts along dimension 1
- grad_rates: float32 [2, 48], P('section', ('groups', 'mp')), parts along dimension 1
The draws below stay inside these ranges and needn't reach their ends.
There are 2 independent parts, one for each index of `groups`. The reference program is written for one: setup_inputs(seed, part) draws one part's arguments, and reference() takes and returns one part's arrays. A program takes and returns all parts, laid end to end along the dimension named above; an argument that names none is the same for every part. Nothing has to cross between parts.
All inputs are finite; a program needn't handle non-finite values. No bound on the sum of `resets` on one device may be relied on, other than what follows from the above.
Results may differ from the reference program's by a relative error of at most 0.018.
Values may be sent and summed in bfloat16 or wider, within the bound.
No kernel may reach another device: no remote copies, remote signals or barrier semaphores. Data moves between devices by JAX's collectives and lax.ppermute only.
A program may use at most 64 MiB of HBM per device.

```python
import math
import jax
import jax.numpy as jnp
from jax import lax

D = 768
E = 1536
N = 16
TOK_DEV = 128
H = 24
TOKENS = 512
SECTIONS = 2
N_SECTION = 2


def set_ends(entries, stream_key, low, largest):
    extent = entries.shape
    index_at = [jax.random.randint(jax.random.fold_in(stream_key, axis), (), 0, extent[axis]) for axis in range(len(extent))]
    entries = entries.at[tuple(index_at)].set(low)
    longest = extent.index(max(extent))
    index_at[longest] = (index_at[longest] + 1) % extent[longest]
    return entries.at[tuple(index_at)].set(largest)


def block_levels(stream_key, shape, cuts, smallest, high):
    gain = 1.0
    for position, parts in cuts:
        heights = jax.random.uniform(jax.random.fold_in(jax.random.fold_in(stream_key, 6), position), (parts,), jnp.float32, smallest / len(cuts), high / len(cuts))
        gain = gain * jnp.repeat(jnp.exp(heights), shape[position] // parts).reshape((-1,) + (1,) * (len(shape) - 1 - position))
    return gain


def normal_values(key, extent, scale, limit, shards=(), held_as=jnp.bfloat16):
    factor_of = block_levels(key, extent, shards, -0.22, 0.18) if shards else 1.0
    values = jax.random.normal(key, extent, jnp.float32) * scale * factor_of
    return jnp.minimum(jnp.maximum(values, -limit), limit).astype(held_as)


def setup_inputs(seed: int = 0, part: int = 0) -> dict:
    seeds = jax.random.split(jax.random.key(seed), 8)
    part_keys = jax.random.split(jax.random.fold_in(seeds[7], part), 8)
    return {
        "section_inputs": normal_values(part_keys[0], (SECTIONS, TOKENS, D), 1.0, 6.0, ((0, 2), (1, 4))),
        "cotangent": normal_values(part_keys[1], (TOKENS, D), 1.0, 6.0, ((0, 4),)),
        "w_in": normal_values(seeds[2], (SECTIONS, D, E), D ** -0.5, 0.21875, ((0, 2), (2, 2))),
        "w_bc": normal_values(seeds[3], (SECTIONS, D, 2 * N), D ** -0.5, 0.21875, ((0, 2),)),
        "w_out": normal_values(seeds[4], (SECTIONS, E, D), E ** -0.5, 0.15625, ((0, 2), (1, 2))),
        "decay_rates": jnp.clip(jnp.exp(math.log(0.05) - 5.5451774 * jax.random.uniform(seeds[5], (SECTIONS, H), jnp.float32) ** block_levels(seeds[5], (SECTIONS, H), ((0, 2), (1, 2)), -0.2, 0.2)), 0.0001953125, 0.05),
        "resets": set_ends((jax.random.randint(part_keys[6], (TOKENS,), 0, 128) < 1).astype(jnp.int32), jax.random.fold_in(part_keys[6], 1), 0, 1),
    }


highest = lax.Precision.HIGHEST
retain_inside_segment = 0.6

def forward_over_span(inner_f, coef_f, speed_real_number, restart_real_mask, state_in):
    tokens_here = inner_f.shape[0]
    channels = inner_f.shape[1]
    head_count = speed_real_number.shape[0]
    head_width = channels // head_count
    states = coef_f.shape[1] // 2
    logarithmic_fade_increment = restart_real_mask[:, None] * jnp.log(retain_inside_segment) - speed_real_number[None, :]
    cumulative_log_decay = jnp.cumsum(logarithmic_fade_increment, axis=0)
    in_scale = jnp.sqrt(-jnp.expm1(-2.0 * speed_real_number))
    b_part = coef_f[:, :states]
    c_part = coef_f[:, states:]
    scores = jnp.dot(c_part, b_part.T, precision=highest)
    sequence_place = jnp.arange(tokens_here)
    causal = sequence_place[:, None] >= sequence_place[None, :]
    cum_heads = cumulative_log_decay.T
    log_gaps = jnp.where(causal[None], cum_heads[:, :, None] - cum_heads[:, None, :], -10000.0)
    weights = jnp.exp(log_gaps) * scores[None]
    scaled = inner_f.reshape(tokens_here, head_count, head_width) * in_scale[None, :, None]
    intra = jnp.einsum('hts,shp->thp', weights, scaled, precision=highest).reshape(tokens_here, channels)
    growth = jnp.repeat(jnp.exp(cumulative_log_decay), head_width, axis=1)
    mixed_out = intra + growth * jnp.dot(c_part, state_in, precision=highest)
    tail_weight = jnp.repeat(jnp.exp(cumulative_log_decay[-1][None, :] - cumulative_log_decay), head_width, axis=1)
    state_out = growth[-1][None, :] * state_in + jnp.dot(b_part.T, tail_weight * scaled.reshape(tokens_here, channels), precision=highest)
    return (mixed_out, state_out)

def full_scan(inner_f, coef_f, speed_real_number, restart_real_mask):
    channels = inner_f.shape[1]
    block_len = min(TOK_DEV, 128)
    blocks = TOKENS // block_len
    inner_blocks = inner_f.reshape(blocks, block_len, channels)
    coef_blocks = coef_f.reshape(blocks, block_len, coef_f.shape[1])
    reset_blocks = restart_real_mask.reshape(blocks, block_len)

    def advance(state_now, pieces):
        mixed_out, state_next = forward_over_span(pieces[0], pieces[1], speed_real_number, pieces[2], state_now)
        return (state_next, mixed_out)
    start = jnp.zeros((coef_f.shape[1] // 2, channels), jnp.float32)
    _, mixed_all = lax.scan(advance, start, (inner_blocks, coef_blocks, reset_blocks))
    return mixed_all.reshape(TOKENS, channels)

def reference(section_inputs, cotangent, w_in, w_bc, w_out, decay_rates, resets):
    restart_real_mask = resets.astype(jnp.float32)
    incoming = cotangent
    grads_in = [None] * N_SECTION
    grads_bc = [None] * N_SECTION
    grads_rate = [None] * N_SECTION
    for layer_index in reversed(range(N_SECTION)):
        layer_activation_values = section_inputs[layer_index]
        inner_act = jnp.dot(layer_activation_values, w_in[layer_index], preferred_element_type=jnp.float32).astype(jnp.bfloat16)
        coef_bc = jnp.dot(layer_activation_values, w_bc[layer_index], preferred_element_type=jnp.float32)
        grad_mixed = lax.dot_general(incoming, w_out[layer_index], (((1,), (1,)), ((), ())), preferred_element_type=jnp.float32)
        _, pullback = jax.vjp(lambda inner_f, coef_f, speed_real_number: full_scan(inner_f, coef_f, speed_real_number, restart_real_mask), inner_act.astype(jnp.float32), coef_bc, decay_rates[layer_index])
        grad_inner, coefficient_adjoint_term, grad_rate = pullback(grad_mixed)
        back_term = lax.dot_general(grad_inner.astype(jnp.bfloat16), w_in[layer_index], (((1,), (1,)), ((), ())), preferred_element_type=jnp.float32)
        back_term = back_term + lax.dot_general(coefficient_adjoint_term.astype(jnp.bfloat16), w_bc[layer_index], (((1,), (1,)), ((), ())), preferred_element_type=jnp.float32)
        result = (incoming.astype(jnp.float32) + back_term).astype(jnp.bfloat16)
        grads_in[layer_index] = result
        grads_bc[layer_index] = jnp.dot(layer_activation_values.astype(jnp.float32).T, coefficient_adjoint_term, precision=highest)
        grads_rate[layer_index] = grad_rate
        incoming = result
    return (jnp.stack(grads_in), jnp.stack(grads_bc), jnp.stack(grads_rate))
```

```python
import functools
import math

import jax
import jax.numpy as jnp
from jax import lax
from jax.experimental import pallas as pl
from jax.experimental.pallas import tpu as pltpu
from jax.sharding import PartitionSpec as P

LOG_KEEP = math.log(0.6)
F32 = jnp.float32
BF16 = jnp.bfloat16

NN = (((1,), (0,)), ((), ()))
NT = (((1,), (1,)), ((), ()))
TN = (((0,), (0,)), ((), ()))

RATE, EMID, ATOT, INV, COUNT = 0, 1, 2, 3, 4
TABLE_ROWS = 8


def mm(a, b, dims):
    return lax.dot_general(a, b, dims, preferred_element_type=F32)


def rotate(value, axis, by):
    n = lax.axis_size(axis)
    return lax.ppermute(value, axis, [(i, (i + by) % n) for i in range(n)])


def swap(value, axis):
    return rotate(value, axis, 1)


def expm1_small(y):
    return y * (1 + y / 2 * (1 + y / 3 * (1 + y / 4 * (1 + y / 5 * (1 + y / 6)))))


def column(tokens):
    return lax.broadcasted_iota(F32, (tokens, 1), 0) if False else lax.broadcasted_iota(
        jnp.int32, (tokens, 1), 0
    ).astype(F32)


def tril_mask(tokens):
    t = lax.broadcasted_iota(jnp.int32, (tokens, tokens), 0)
    s = lax.broadcasted_iota(jnp.int32, (tokens, tokens), 1)
    return t, s


def call(kernel, outs, args, *, smem=(), flops=0, bytes_accessed=0, name=None):
    return pl.pallas_call(
        kernel,
        out_shape=[jax.ShapeDtypeStruct(s, d) for s, d in outs],
        in_specs=[
            pl.BlockSpec(memory_space=pltpu.SMEM if i in smem else pltpu.VMEM)
            for i in range(len(args))
        ],
        out_specs=[pl.BlockSpec(memory_space=pltpu.VMEM) for _ in outs],
        compiler_params=pltpu.CompilerParams(vmem_limit_bytes=24 << 20),
        cost_estimate=pl.CostEstimate(
            flops=flops, bytes_accessed=bytes_accessed, transcendentals=0
        ),
        name=name,
    )(*args)


def start_kernel(
    seq_size,
    x_ref,
    g_ref,
    w_in_ref,
    w_bc_ref,
    w_out_ref,
    rates_ref,
    resets_ref,
    up_ref,
    gmp_ref,
    coef_ref,
    a_ref,
    sa_ref,
    table_ref,
    *pay_refs,
):
    tokens = x_ref.shape[1]
    channels = w_in_ref.shape[2]
    heads = rates_ref.shape[1]
    width = channels // heads
    states = w_bc_ref.shape[2] // 2
    x = x_ref[0]
    gm = mm(g_ref[...], w_out_ref[0], NT)
    coef = mm(x, w_bc_ref[0], NN)
    inner = mm(x, w_in_ref[0], NN).astype(BF16).astype(F32)

    lane_head = lax.broadcasted_iota(jnp.int32, (1, channels), 1) // width
    rate = jnp.zeros((1, channels), F32)
    for k in range(heads):
        rate = jnp.where(lane_head == k, rates_ref[0, k], rate)
    t, s = tril_mask(tokens)
    resets = resets_ref[...].astype(F32)
    count = jnp.sum(jnp.where(s <= t, resets, 0.0), axis=1, keepdims=True)
    log = count * LOG_KEEP - (column(tokens) + 1.0) * rate
    mid = log[tokens // 2 - 1 : tokens // 2, :]
    a = jnp.exp(log - mid)
    growth = expm1_small(2.0 * rate)
    scale = jnp.sqrt(growth / (1.0 + growth))
    emid = jnp.exp(mid)
    atot = a[tokens - 1 : tokens, :]
    up = (inner * (scale / a)).astype(BF16)
    gmp = (gm * a).astype(BF16)
    coef_b = coef.astype(BF16)
    up_ref[...] = up
    gmp_ref[...] = gmp
    coef_ref[...] = coef_b
    a_ref[...] = a
    sa_ref[...] = scale / a
    total = jnp.broadcast_to(count[tokens - 1 : tokens, :], (1, channels))
    table_ref[...] = jnp.concatenate(
        [rate, emid, atot, 1.0 / growth, total, jnp.zeros((TABLE_ROWS - 5, channels), F32)], axis=0
    )
    both = mm(coef_b, up, TN)
    state = atot * both[:states, :]
    both = mm(coef_b, gmp, TN)
    adjoint = emid * both[states:, :]
    me = lax.axis_index("seq")
    tail = jnp.broadcast_to(total, (8, channels))
    for k in range(1, seq_size):
        forward = me + k < seq_size
        data = jnp.where(forward, state, adjoint)
        pay_refs[k - 1][...] = jnp.concatenate([data, tail], axis=0).astype(BF16)


def local_kernel(up_ref, gmp_ref, coef_ref, gu_ref, gcoef_ref, lag_ref):
    tokens = up_ref.shape[0]
    states = coef_ref.shape[1] // 2
    up, gmp = up_ref[...], gmp_ref[...]
    coef = coef_ref[...]
    b_part, c_part = coef[:, :states], coef[:, states:]
    t, s = tril_mask(tokens)
    causal = s <= t
    scores = jnp.where(causal, mm(c_part, b_part, NT), 0.0)
    gu_ref[...] = mm(scores.astype(BF16), gmp, TN)
    lagged = (scores * (t - s).astype(F32)).astype(BF16)
    lag_ref[...] = jnp.sum(gmp.astype(F32) * mm(lagged, up, NN), axis=0, keepdims=True)
    gs = jnp.where(causal, mm(gmp, up, NT), 0.0).astype(BF16)
    gcoef_ref[...] = jnp.concatenate([mm(gs, c_part, TN), mm(gs, b_part, NN)], axis=1)


def unpack(seq_size, recv_refs, table_ref, states, tokens):
    channels = table_ref.shape[1]
    rate = table_ref[RATE : RATE + 1, :]
    me = lax.axis_index("seq")
    source = [lax.rem(me - k + seq_size, seq_size) for k in range(1, seq_size)]
    data = [r[...].astype(F32) for r in recv_refs]
    gap = [d[states : states + 1, :] * LOG_KEEP - tokens * rate for d in data]
    h_in = jnp.zeros((states, channels), F32)
    adj = jnp.zeros((states, channels), F32)
    weights = []
    for i, src in enumerate(source):
        forward = src < me
        low, high = jnp.minimum(src, me), jnp.maximum(src, me)
        log = jnp.zeros((1, channels), F32)
        for j, other in enumerate(source):
            if j != i:
                between = jnp.logical_and(other > low, other < high)
                log = log + jnp.where(between, gap[j], 0.0)
        weight = jnp.exp(log)
        term = weight * data[i][:states, :]
        h_in = h_in + jnp.where(forward, term, 0.0)
        adj = adj + jnp.where(forward, 0.0, term)
        weights.append(jnp.where(forward, 0.0, weight))
    return h_in, adj, weights


def finish(
    adj, hpp, gu, gcoef, lag, up_ref, gmp_ref, coef_ref, sa_ref, table_ref, x_ref, w_in_ref, w_bc_ref
):
    tokens, channels = up_ref.shape
    states = coef_ref.shape[1] // 2
    up, gmp, coef = up_ref[...], gmp_ref[...], coef_ref[...]
    atot = table_ref[ATOT : ATOT + 1, :]
    adjp = atot * adj
    zero = jnp.zeros((states, channels), BF16)
    adj_rows = jnp.concatenate([adjp.astype(BF16), zero], axis=0)
    h_rows = jnp.concatenate([zero, hpp.astype(BF16)], axis=0)
    v = mm(coef, adj_rows, NN)
    ch = mm(coef, h_rows, NN)
    gu = gu + v
    grad_inner = (sa_ref[...] * gu).astype(BF16)
    gcoef = (gcoef + mm(up, adj_rows, NT) + mm(gmp, h_rows, NT)).astype(BF16)
    back = mm(grad_inner, w_in_ref[0], NT) + mm(gcoef, w_bc_ref[0], NT)
    place = column(tokens)
    up_f, gmp_f = up.astype(F32), gmp.astype(F32)
    lag = (
        lag
        + jnp.sum(gmp_f * ((place + 1.0) * ch), axis=0, keepdims=True)
        + jnp.sum(up_f * ((tokens - 1.0 - place) * v), axis=0, keepdims=True)
        + tokens * jnp.sum(hpp * adjp, axis=0, keepdims=True)
    )
    total = jnp.sum(up_f * gu, axis=0, keepdims=True)
    rate_row = total * table_ref[INV : INV + 1, :] - lag
    dw = mm(gcoef, x_ref[0], TN)
    reduced = jnp.concatenate([dw, jnp.broadcast_to(rate_row, (8, channels))], axis=0)
    return back, reduced


def first_finish_kernel(
    seq_size,
    up_ref,
    gmp_ref,
    coef_ref,
    sa_ref,
    table_ref,
    x_ref,
    w_in_ref,
    w_bc_ref,
    gu_ref,
    gcoef_ref,
    lag_ref,
    g_ref,
    *refs,
):
    recv_refs, (send_ref, keep_ref, red_ref, hpp_ref, weight_ref) = (
        refs[: seq_size - 1],
        refs[seq_size - 1 :],
    )
    tokens = up_ref.shape[0]
    states = coef_ref.shape[1] // 2
    h_in, adj, weights = unpack(seq_size, recv_refs, table_ref, states, tokens)
    hpp = table_ref[EMID : EMID + 1, :] * h_in
    hpp_ref[...] = hpp
    for k, weight in enumerate(weights):
        weight_ref[k : k + 1, :] = weight
    back, red_ref[...] = finish(
        adj,
        hpp,
        gu_ref[...],
        gcoef_ref[...],
        lag_ref[...],
        up_ref,
        gmp_ref,
        coef_ref,
        sa_ref,
        table_ref,
        x_ref,
        w_in_ref,
        w_bc_ref,
    )
    split(back, g_ref[...], send_ref, keep_ref)


def split(back, g, send_ref, keep_ref):
    half = back.shape[1] // 2
    low = lax.axis_index("mp") == 0
    send_ref[...] = jnp.where(low, back[:, half:], back[:, :half]).astype(BF16)
    own = jnp.where(low, back[:, :half], back[:, half:])
    keep_ref[...] = own + jnp.where(low, g[:, :half], g[:, half:]).astype(F32)


def joined(mine, other):
    low = lax.axis_index("mp") == 0
    return jnp.concatenate([jnp.where(low, mine, other), jnp.where(low, other, mine)], axis=1)


def gather_adjoint(recv_refs, weight_ref):
    adj = None
    for k, r in enumerate(recv_refs):
        term = weight_ref[k : k + 1, :] * r[...].astype(F32)
        adj = term if adj is None else adj + term
    return adj


def hop_kernel(
    mine_ref, other_ref, w_out_ref, coef_ref, a_ref, table_ref, gmp_ref, adjoint_ref
):
    states = coef_ref.shape[1] // 2
    g = joined(mine_ref[...], other_ref[...])
    gmp = (a_ref[...] * mm(g, w_out_ref[0], NT)).astype(BF16)
    gmp_ref[...] = gmp
    both = mm(coef_ref[...], gmp, TN)
    adjoint_ref[...] = (table_ref[EMID : EMID + 1, :] * both[states:, :]).astype(BF16)


def middle_finish_kernel(
    seq_size,
    up_ref,
    gmp_ref,
    coef_ref,
    sa_ref,
    table_ref,
    x_ref,
    w_in_ref,
    w_bc_ref,
    gu_ref,
    gcoef_ref,
    lag_ref,
    mine_ref,
    other_ref,
    hpp_ref,
    weight_ref,
    *refs,
):
    recv_refs, (send_ref, keep_ref, red_ref) = refs[: seq_size - 1], refs[seq_size - 1 :]
    back, red_ref[...] = finish(
        gather_adjoint(recv_refs, weight_ref),
        hpp_ref[...],
        gu_ref[...],
        gcoef_ref[...],
        lag_ref[...],
        up_ref,
        gmp_ref,
        coef_ref,
        sa_ref,
        table_ref,
        x_ref,
        w_in_ref,
        w_bc_ref,
    )
    split(back, joined(mine_ref[...], other_ref[...]), send_ref, keep_ref)


def last_finish_kernel(
    seq_size,
    up_ref,
    gmp_ref,
    coef_ref,
    sa_ref,
    table_ref,
    x_ref,
    w_in_ref,
    w_bc_ref,
    gu_ref,
    gcoef_ref,
    lag_ref,
    kept_half_ref,
    kept_red_ref,
    hpp_ref,
    weight_ref,
    *refs,
):
    recv_refs, (part_ref, red_ref) = refs[: seq_size - 1], refs[seq_size - 1 :]
    back, red = finish(
        gather_adjoint(recv_refs, weight_ref),
        hpp_ref[...],
        gu_ref[...],
        gcoef_ref[...],
        lag_ref[...],
        up_ref,
        gmp_ref,
        coef_ref,
        sa_ref,
        table_ref,
        x_ref,
        w_in_ref,
        w_bc_ref,
    )
    active = lax.axis_index("section") == 0
    low = lax.axis_index("mp") == 0
    half = kept_half_ref[...]
    zero = jnp.zeros_like(half)
    done = jnp.concatenate([jnp.where(low, half, zero), jnp.where(low, zero, half)], axis=1)
    part_ref[...] = jnp.where(active, back.astype(BF16), done)
    red_ref[...] = jnp.where(active, red, kept_red_ref[...]).astype(BF16)


def output_kernel(part_ref, part2_ref, mine_ref, other_ref, red_ref, red2_ref, out_ref, sum_ref):
    active = lax.axis_index("section") == 0
    g = joined(mine_ref[...], other_ref[...]).astype(F32)
    g = jnp.where(active, g, 0.0)
    out_ref[0] = (g + (part_ref[...].astype(F32) + part2_ref[...].astype(F32))).astype(BF16)
    rows = red_ref.shape[0]
    own, other = red_ref[...].astype(F32), red2_ref[...].astype(F32)
    is_rate = lax.broadcasted_iota(jnp.int32, (rows, 1), 0) >= rows - 8
    sum_ref[...] = jnp.where(is_rate, own, own + other).astype(BF16)


def total_kernel(seq_size, heads, *refs):
    pieces, (w_ref, rate_ref) = refs[:seq_size], refs[seq_size:]
    me = lax.axis_index("seq")
    data = [r[...].astype(F32) for r in pieces]
    source = [lax.rem(me - k + seq_size, seq_size) for k in range(seq_size)]
    total = None
    for j in range(seq_size):
        term = data[0]
        for k in range(1, seq_size):
            term = jnp.where(source[k] == j, data[k], term)
        total = term if total is None else total + term
    rows, channels = total.shape
    w_ref[0] = total[: rows - 8, :].T
    width = channels // heads
    row = total[rows - 8 : rows - 7, :]
    lane = lax.broadcasted_iota(jnp.int32, (heads, channels), 1) // width
    head = lax.broadcasted_iota(jnp.int32, (heads, channels), 0)
    rate_ref[...] = jnp.sum(jnp.where(lane == head, row, 0.0), axis=1, keepdims=True)


def shards(section_inputs, cotangent, w_in, w_bc, w_out, decay_rates, resets):
    tokens, width = cotangent.shape
    channels = w_in.shape[2]
    coefs = w_bc.shape[2]
    states = coefs // 2
    heads = decay_rates.shape[1]
    seq_size = lax.axis_size("seq")
    sections = lax.axis_size("section")
    half = width // 2
    big = 2 * tokens * width * channels
    vec = ((tokens, channels), F32)

    up, gmp, coef, a, sa, table, *pay = call(
        functools.partial(start_kernel, seq_size),
        [
            ((tokens, channels), BF16),
            ((tokens, channels), BF16),
            ((tokens, coefs), BF16),
            vec,
            vec,
            ((TABLE_ROWS, channels), F32),
        ]
        + [((states + 8, channels), BF16)] * (seq_size - 1),
        [
            section_inputs,
            cotangent,
            w_in,
            w_bc,
            w_out,
            decay_rates,
            resets.reshape(1, tokens),
        ],
        smem=(5,),
        flops=2 * big,
        bytes_accessed=4 * width * channels,
        name="start",
    )
    recv = [rotate(p, "seq", k + 1) for k, p in enumerate(pay)]

    def local(gradient):
        return call(
            local_kernel,
            [vec, ((tokens, coefs), F32), ((1, channels), F32)],
            [up, gradient, coef],
            flops=big,
            bytes_accessed=4 * tokens * channels,
            name="local",
        )

    shared = lambda gradient: [up, gradient, coef, sa, table, section_inputs, w_in, w_bc]
    reduced = ((coefs + 8, channels), F32)
    section = lax.axis_index("section")
    send, keep, red, hpp, weight = call(
        functools.partial(first_finish_kernel, seq_size),
        [
            ((tokens, half), BF16),
            ((tokens, half), F32),
            reduced,
            ((states, channels), F32),
            ((seq_size - 1, channels), F32),
        ],
        [*shared(gmp), *local(gmp), cotangent, *recv],
        flops=big,
        bytes_accessed=2 * width * channels,
        name="first",
    )
    kept_half, kept_red = None, None
    for moment in range(1, sections):
        half_result = (keep + swap(send, "mp").astype(F32)).astype(BF16)
        was_active = section == sections - moment
        if kept_half is None:
            kept_half, kept_red = half_result, red
        else:
            kept_half = jnp.where(was_active, half_result, kept_half)
            kept_red = jnp.where(was_active, red, kept_red)
        mine = rotate(half_result, "section", -1)
        other = swap(mine, "mp")
        gmp, adjoint = call(
            hop_kernel,
            [((tokens, channels), BF16), ((states, channels), BF16)],
            [mine, other, w_out, coef, a, table],
            flops=big,
            bytes_accessed=2 * width * channels,
            name="hop",
        )
        recv = [rotate(adjoint, "seq", k) for k in range(1, seq_size)]
        if moment < sections - 1:
            send, keep, red = call(
                functools.partial(middle_finish_kernel, seq_size),
                [((tokens, half), BF16), ((tokens, half), F32), reduced],
                [*shared(gmp), *local(gmp), mine, other, hpp, weight, *recv],
                flops=big,
                bytes_accessed=2 * width * channels,
                name="middle",
            )
    part, red = call(
        functools.partial(last_finish_kernel, seq_size),
        [((tokens, width), BF16), ((coefs + 8, channels), BF16)],
        [*shared(gmp), *local(gmp), kept_half, kept_red, hpp, weight, *recv],
        flops=big,
        bytes_accessed=2 * width * channels,
        name="last",
    )
    out, red = call(
        output_kernel,
        [((1, tokens, width), BF16), ((coefs + 8, channels), BF16)],
        [part, swap(part, "mp"), mine, other, red, swap(red, "mp")],
        name="output",
    )
    grad_w, grad_rates = call(
        functools.partial(total_kernel, seq_size, heads),
        [((1, width, coefs), F32), ((heads, 1), F32)],
        [red] + [rotate(red, "seq", k) for k in range(1, seq_size)],
        name="total",
    )
    return out, grad_w, grad_rates.reshape(1, heads)


def solution(mesh):
    return jax.shard_map(
        shards,
        mesh=mesh,
        in_specs=(
            P("section", ("groups", "seq"), None),
            P(("groups", "seq"), None),
            P("section", None, "mp"),
            P("section", None, None),
            P("section", "mp", None),
            P("section", "mp"),
            P(("groups", "seq")),
        ),
        out_specs=(
            P("section", ("groups", "seq"), None),
            P("section", "groups", None),
            P("section", ("groups", "mp")),
        ),
        check_vma=False,
    )
```

```python
import functools
import math

import jax
import jax.numpy as jnp
from jax import lax
from jax.experimental import pallas as pl
from jax.experimental.pallas import tpu as pltpu
from jax.sharding import PartitionSpec as P

LOG_KEEP = math.log(0.6)
F32 = jnp.float32
BF16 = jnp.bfloat16

NN = (((1,), (0,)), ((), ()))
NT = (((1,), (1,)), ((), ()))
TN = (((0,), (0,)), ((), ()))

RATE, EMID, ATOT, INV, COUNT = 0, 1, 2, 3, 4
TABLE_ROWS = 8
OUT_CHUNKS, IN_CHUNKS = 2, 2


def mm(a, b, dims):
    return lax.dot_general(a, b, dims, preferred_element_type=F32)


def rotate(value, axis, by):
    n = lax.axis_size(axis)
    return lax.ppermute(value, axis, [(i, (i + by) % n) for i in range(n)])


def partner(value, axis, k):
    n = lax.axis_size(axis)
    return lax.ppermute(value, axis, [(i, i ^ k) for i in range(n)])


def swap(value, axis):
    return rotate(value, axis, 1)


def expm1_small(y):
    return y * (1 + y / 2 * (1 + y / 3 * (1 + y / 4 * (1 + y / 5 * (1 + y / 6)))))


def column(tokens):
    return lax.broadcasted_iota(jnp.int32, (tokens, 1), 0).astype(F32)


def tril_mask(tokens):
    t = lax.broadcasted_iota(jnp.int32, (tokens, tokens), 0)
    s = lax.broadcasted_iota(jnp.int32, (tokens, tokens), 1)
    return t, s


def call(kernel, outs, args, *, space=pltpu.VMEM, scratch=(), flops=0, bytes_accessed=0, name=None):
    if space is pltpu.HBM:
        args = [pltpu.with_memory_space_constraint(a, space) for a in args]
    return pl.pallas_call(
        kernel,
        out_shape=[jax.ShapeDtypeStruct(s, d) for s, d in outs],
        in_specs=[pl.BlockSpec(memory_space=space) for _ in args],
        out_specs=[pl.BlockSpec(memory_space=pltpu.VMEM) for _ in outs],
        scratch_shapes=list(scratch),
        compiler_params=pltpu.CompilerParams(vmem_limit_bytes=24 << 20),
        cost_estimate=pl.CostEstimate(
            flops=flops, bytes_accessed=bytes_accessed, transcendentals=0
        ),
        name=name,
    )(*args)


def start_kernel(
    seq_size,
    x_hbm,
    g_hbm,
    w_in_hbm,
    w_bc_hbm,
    w_out_hbm,
    rates_hbm,
    resets_hbm,
    up_ref,
    gmp_ref,
    coef_ref,
    a_ref,
    sa_ref,
    table_ref,
    *refs,
):
    pay_refs = refs[: seq_size - 1]
    x_ref, g_ref, w_in_ref, w_bc_ref, w_out_ref, rates_ref, resets_ref, small_sem, wide_sem = refs[
        seq_size - 1 :
    ]
    tokens = x_hbm.shape[1]
    channels = w_in_hbm.shape[2]
    heads = rates_hbm.shape[1]
    width = channels // heads
    states = w_bc_hbm.shape[1] // 2
    small = [
        pltpu.make_async_copy(src, dst, small_sem.at[i])
        for i, (src, dst) in enumerate(
            [
                (rates_hbm, rates_ref),
                (resets_hbm, resets_ref),
                (g_hbm, g_ref),
                (x_hbm.at[0], x_ref),
                (w_bc_hbm.at[0], w_bc_ref),
            ]
        )
    ]
    rows, cols = channels // OUT_CHUNKS, channels // IN_CHUNKS
    out_parts = [slice(c * rows, (c + 1) * rows) for c in range(OUT_CHUNKS)]
    in_parts = [slice(c * cols, (c + 1) * cols) for c in range(IN_CHUNKS)]
    from_out = [
        pltpu.make_async_copy(w_out_hbm.at[0, p, :], w_out_ref.at[p, :], wide_sem.at[i])
        for i, p in enumerate(out_parts)
    ]
    from_in = [
        pltpu.make_async_copy(w_in_hbm.at[0, :, p], w_in_ref.at[:, p], wide_sem.at[OUT_CHUNKS + i])
        for i, p in enumerate(in_parts)
    ]
    for copy in small[:3] + from_out + small[3:] + from_in:
        copy.start()
    small[0].wait()
    small[1].wait()

    lane_head = lax.broadcasted_iota(jnp.int32, (1, channels), 1) // width
    rate = jnp.zeros((1, channels), F32)
    for k in range(heads):
        rate = jnp.where(lane_head == k, rates_ref[0, k], rate)
    t, s = tril_mask(tokens)
    resets = resets_ref[...].astype(F32)
    count = jnp.sum(jnp.where(s <= t, resets, 0.0), axis=1, keepdims=True)
    log = count * LOG_KEEP - (column(tokens) + 1.0) * rate
    mid = log[tokens // 2 - 1 : tokens // 2, :]
    a = jnp.exp(log - mid)
    growth = expm1_small(2.0 * rate)
    scale = jnp.sqrt(growth / (1.0 + growth))
    emid = jnp.exp(mid)
    atot = a[tokens - 1 : tokens, :]
    a_ref[...] = a
    total = jnp.broadcast_to(count[tokens - 1 : tokens, :], (1, channels))
    table_ref[...] = jnp.concatenate(
        [rate, emid, atot, 1.0 / growth, total, jnp.zeros((TABLE_ROWS - 5, channels), F32)], axis=0
    )

    small[2].wait()
    g = g_ref[...]
    for copy, part in zip(from_out, out_parts):
        copy.wait()
        gmp_ref[:, part] = (mm(g, w_out_ref[part, :], NT) * a[:, part]).astype(BF16)
    small[3].wait()
    small[4].wait()
    x = x_ref[...]
    coef = mm(x, w_bc_ref[...], NT).astype(BF16)
    coef_ref[...] = coef
    adjoint = emid * mm(coef, gmp_ref[...], TN)[states:, :]
    sa = scale / a
    sa_ref[...] = sa
    state = []
    for copy, part in zip(from_in, in_parts):
        copy.wait()
        inner = mm(x, w_in_ref[:, part], NN)
        up = (inner.astype(BF16).astype(F32) * sa[:, part]).astype(BF16)
        up_ref[:, part] = up
        state.append(atot[:, part] * mm(coef, up, TN)[:states, :])
    state = jnp.concatenate(state, axis=1)
    me = lax.axis_index("seq")
    tail = jnp.broadcast_to(count[tokens - 1 : tokens, :], (states, 128)).astype(BF16)
    for k in range(1, seq_size):
        forward = (me ^ k) > me
        pay_refs[k - 1][:, :channels] = jnp.where(forward, state, adjoint).astype(BF16)
        pay_refs[k - 1][:, channels:] = tail


def split(value):
    half = value.shape[1] // 2
    low = lax.axis_index("mp") == 0
    left, right = value[:, :half], value[:, half:]
    return jnp.where(low, left, right), jnp.where(low, right, left)


def joined(mine, other):
    low = lax.axis_index("mp") == 0
    return jnp.concatenate([jnp.where(low, mine, other), jnp.where(low, other, mine)], axis=1)


def coef_grads(gs, b_part, c_part):
    return jnp.concatenate([mm(gs, c_part, TN), mm(gs, b_part, NN)], axis=1)


def local_kernel(up_ref, gmp_ref, coef_ref, gu_ref, gcoef_ref, lag_ref):
    tokens = up_ref.shape[0]
    states = coef_ref.shape[1] // 2
    up, gmp = up_ref[...], gmp_ref[...]
    coef = coef_ref[...]
    b_part, c_part = coef[:, :states], coef[:, states:]
    t, s = tril_mask(tokens)
    causal = s <= t
    scores = jnp.where(causal, mm(c_part, b_part, NT), 0.0)
    gu_ref[...] = mm(scores.astype(BF16), gmp, TN)
    lagged = (scores * (t - s).astype(F32)).astype(BF16)
    lag_ref[...] = jnp.sum(gmp.astype(F32) * mm(lagged, up, NN), axis=0, keepdims=True)
    gs = jnp.where(causal, mm(gmp, up, NT), 0.0).astype(BF16)
    gcoef_ref[...] = coef_grads(gs, b_part, c_part)


def unpack(seq_size, recv_refs, table_ref, states, tokens):
    channels = table_ref.shape[1]
    rate = table_ref[RATE : RATE + 1, :]
    me = lax.axis_index("seq")
    source = [me ^ k for k in range(1, seq_size)]
    data = [r[:, :channels].astype(F32) for r in recv_refs]
    gap = [
        r[:1, channels : channels + 1].astype(F32) * LOG_KEEP - tokens * rate for r in recv_refs
    ]
    h_in = jnp.zeros((states, channels), F32)
    adj = jnp.zeros((states, channels), F32)
    weights = []
    for i, src in enumerate(source):
        forward = src < me
        low, high = jnp.minimum(src, me), jnp.maximum(src, me)
        log = jnp.zeros((1, channels), F32)
        for j, other in enumerate(source):
            if j != i:
                between = jnp.logical_and(other > low, other < high)
                log = log + jnp.where(between, gap[j], 0.0)
        weight = jnp.exp(log)
        term = weight * data[i]
        h_in = h_in + jnp.where(forward, term, 0.0)
        adj = adj + jnp.where(forward, 0.0, term)
        weights.append(jnp.where(forward, 0.0, weight))
    return h_in, adj, weights


def state_rows(hpp):
    return jnp.concatenate([jnp.zeros_like(hpp), hpp], axis=0).astype(BF16)


def input_gradient(rows, gu, gcoef, coef, sa_ref, w_in_ref, w_bc_ref):
    grad_inner = (sa_ref[...] * (gu + mm(coef, rows, NN))).astype(BF16)
    return mm(grad_inner, w_in_ref[0], NT) + mm(gcoef, w_bc_ref[0], NN)


def adjoint_rows(adj, table_ref):
    adjp = table_ref[ATOT : ATOT + 1, :] * adj
    return jnp.concatenate([adjp, jnp.zeros_like(adjp)], axis=0).astype(BF16)


def coef_total(rows, h_rows, gcoef_ref, up, gmp):
    return (gcoef_ref[...] + mm(gmp, h_rows, NT) + mm(up, rows, NT)).astype(BF16)


def parameter_gradients(
    adj, hpp, gu_ref, gcoef_ref, lag_ref, up_ref, gmp_ref, coef_ref, table_ref, x_ref
):
    tokens, channels = up_ref.shape
    up, gmp, coef = up_ref[...], gmp_ref[...], coef_ref[...]
    adjp = table_ref[ATOT : ATOT + 1, :] * adj
    rows, h_rows = adjoint_rows(adj, table_ref), state_rows(hpp)
    gcoef = coef_total(rows, h_rows, gcoef_ref, up, gmp)
    dw = mm(gcoef, x_ref[0], TN)
    v = mm(coef, rows, NN)
    ch = mm(coef, h_rows, NN)
    place = column(tokens)
    up_f, gmp_f = up.astype(F32), gmp.astype(F32)
    lag = (
        lag_ref[...]
        + jnp.sum(gmp_f * ((place + 1.0) * ch), axis=0, keepdims=True)
        + jnp.sum(up_f * ((tokens - 1.0 - place) * v), axis=0, keepdims=True)
        + tokens * jnp.sum(hpp * adjp, axis=0, keepdims=True)
    )
    total = jnp.sum(up_f * (gu_ref[...] + v), axis=0, keepdims=True)
    rate_row = total * table_ref[INV : INV + 1, :] - lag
    red = jnp.concatenate([dw, jnp.broadcast_to(rate_row, (8, channels))], axis=0)
    return red, rows, gcoef


def first_kernel(
    seq_size,
    up_ref,
    gmp_ref,
    coef_ref,
    table_ref,
    sa_ref,
    w_in_ref,
    w_bc_ref,
    gu_ref,
    gcoef_ref,
    g_ref,
    *refs,
):
    recv_refs, (keep_ref, send_ref, adj_ref, hpp_ref, weight_ref) = (
        refs[: seq_size - 1],
        refs[seq_size - 1 :],
    )
    tokens = up_ref.shape[0]
    states = coef_ref.shape[1] // 2
    recv_refs = recv_refs[::-1]
    h_in, adj, weights = unpack(seq_size, recv_refs, table_ref, states, tokens)
    hpp = table_ref[EMID : EMID + 1, :] * h_in
    hpp_ref[...] = hpp
    for k, weight in enumerate(weights):
        weight_ref[k : k + 1, :] = weight
    adj_ref[...] = adj
    rows = adjoint_rows(adj, table_ref)
    gcoef = coef_total(rows, state_rows(hpp), gcoef_ref, up_ref[...], gmp_ref[...])
    back = input_gradient(rows, gu_ref[...], gcoef, coef_ref[...], sa_ref, w_in_ref, w_bc_ref)
    store_split(back, g_ref[...], keep_ref, send_ref)


def store_split(back, g, keep_ref, send_ref):
    keep, send = split(back)
    keep_ref[...] = keep + split(g)[0].astype(F32)
    send_ref[...] = send.astype(BF16)


def gather_adjoint(recv_refs, weight_ref):
    adj = None
    for k, r in enumerate(recv_refs):
        term = weight_ref[k : k + 1, :] * r[...].astype(F32)
        adj = term if adj is None else adj + term
    return adj


def first_parameter_kernel(
    up_ref,
    gmp_ref,
    coef_ref,
    table_ref,
    x_ref,
    gu_ref,
    gcoef_ref,
    lag_ref,
    hpp_ref,
    adj_ref,
    red_ref,
):
    red_ref[...] = parameter_gradients(
        adj_ref[...],
        hpp_ref[...],
        gu_ref,
        gcoef_ref,
        lag_ref,
        up_ref,
        gmp_ref,
        coef_ref,
        table_ref,
        x_ref,
    )[0]


def parameter_kernel(
    last,
    seq_size,
    up_ref,
    gmp_ref,
    coef_ref,
    table_ref,
    x_ref,
    gu_ref,
    gcoef_in_ref,
    lag_ref,
    hpp_ref,
    weight_ref,
    kept_ref,
    *refs,
):
    recv_refs, (rows_ref, gcoef_ref, *out_refs) = refs[: seq_size - 1], refs[seq_size - 1 :]
    red, rows_ref[...], gcoef_ref[...] = parameter_gradients(
        gather_adjoint(recv_refs, weight_ref),
        hpp_ref[...],
        gu_ref,
        gcoef_in_ref,
        lag_ref,
        up_ref,
        gmp_ref,
        coef_ref,
        table_ref,
        x_ref,
    )
    if not last:
        out_refs[0][...] = red
        return
    red = jnp.where(lax.axis_index("section") == 0, red, kept_ref[...])
    keep_ref, send_ref = out_refs
    coefs = red.shape[0] - 8
    half = red.shape[1] // 2
    keep, send = split(red[:coefs, :])
    send_ref[...] = send.astype(BF16)
    keep_ref[:coefs, :] = keep
    rate = red[coefs:, :]
    keep_ref[coefs : coefs + 1, :] = rate[:1, :half]
    keep_ref[coefs + 1 : coefs + 2, :] = rate[:1, half:]
    keep_ref[coefs + 2 :, :] = jnp.zeros((6, half), F32)


def middle_input_kernel(
    rows_ref, gu_ref, gcoef_ref, coef_ref, sa_ref, w_in_ref, w_bc_ref, mine_ref, other_ref, keep_ref, send_ref
):
    back = input_gradient(
        rows_ref[...], gu_ref[...], gcoef_ref[...], coef_ref[...], sa_ref, w_in_ref, w_bc_ref
    )
    store_split(back, joined(mine_ref[...], other_ref[...]), keep_ref, send_ref)


def last_input_kernel(
    rows_ref, gu_ref, gcoef_ref, coef_ref, sa_ref, w_in_ref, w_bc_ref, kept_ref, part_ref
):
    back = input_gradient(
        rows_ref[...], gu_ref[...], gcoef_ref[...], coef_ref[...], sa_ref, w_in_ref, w_bc_ref
    )
    half = kept_ref[...]
    zero = jnp.zeros_like(half)
    low = lax.axis_index("mp") == 0
    done = jnp.concatenate([jnp.where(low, half, zero), jnp.where(low, zero, half)], axis=1)
    part_ref[...] = jnp.where(lax.axis_index("section") == 0, back.astype(BF16), done)


def scaled_gradient(g, w_out_ref, coef, a_ref, table_ref):
    gmp = (a_ref[...] * mm(g, w_out_ref[0], NT)).astype(BF16)
    states = coef.shape[1] // 2
    adjoint = table_ref[EMID : EMID + 1, :] * mm(coef, gmp, TN)[states:, :]
    return gmp, adjoint


def hop_kernel(
    w_out_ref, coef_ref, a_ref, table_ref, mine_ref, other_ref, gmp_ref, adjoint_ref
):
    g = joined(mine_ref[...], other_ref[...])
    gmp, adjoint = scaled_gradient(g, w_out_ref, coef_ref[...], a_ref, table_ref)
    gmp_ref[...] = gmp
    adjoint_ref[...] = adjoint.astype(BF16)


def pair_kernel(keep_ref, other_ref, sum_ref):
    coefs = other_ref.shape[0]
    sum_ref[:coefs, :] = (keep_ref[:coefs, :] + other_ref[...].astype(F32)).astype(BF16)
    sum_ref[coefs:, :] = keep_ref[coefs:, :].astype(BF16)


def total_kernel(seq_size, *refs):
    pieces, (w_ref, rate_ref) = refs[:seq_size], refs[seq_size:]
    heads = rate_ref.shape[1]
    terms = [r[...].astype(F32) for r in pieces]
    while len(terms) > 1:
        terms = [x + y for x, y in zip(terms[::2], terms[1::2])]
    total = terms[0]
    coefs, half = w_ref.shape
    channels = 2 * half
    w_ref[...] = total[:coefs, :]
    row = jnp.concatenate([total[coefs : coefs + 1, :], total[coefs + 1 : coefs + 2, :]], axis=1)
    lane = lax.broadcasted_iota(jnp.int32, (heads, channels), 1) // (channels // heads)
    head = lax.broadcasted_iota(jnp.int32, (heads, channels), 0)
    col = jnp.sum(jnp.where(lane == head, row, 0.0), axis=1, keepdims=True)
    i = lax.broadcasted_iota(jnp.int32, (heads, heads), 0)
    j = lax.broadcasted_iota(jnp.int32, (heads, heads), 1)
    rate_ref[...] = jnp.sum(jnp.where(i == j, col, 0.0), axis=0, keepdims=True)


def output_kernel(part_ref, part2_ref, mine_ref, other_ref, out_ref):
    active = lax.axis_index("section") == 0
    g = jnp.where(active, joined(mine_ref[...], other_ref[...]).astype(F32), 0.0)
    out_ref[0] = (g + (part_ref[...].astype(F32) + part2_ref[...].astype(F32))).astype(BF16)


def join_kernel(mine_ref, other_ref, out_ref):
    out_ref[0] = joined(mine_ref[...], other_ref[...])


def shards(section_inputs, cotangent, w_in, w_bc, w_out, decay_rates, resets):
    tokens, width = cotangent.shape
    channels = w_in.shape[2]
    coefs = w_bc.shape[2]
    w_bc = jnp.swapaxes(w_bc, 1, 2)
    states = coefs // 2
    heads = decay_rates.shape[1]
    seq_size = lax.axis_size("seq")
    sections = lax.axis_size("section")
    others = seq_size - 1
    big = 2 * tokens * width * channels
    vec, low = ((tokens, channels), F32), ((tokens, channels), BF16)
    row = ((1, channels), F32)
    few = ((tokens, coefs), F32)
    reduced = ((coefs + 8, channels), F32)

    up, gmp, coef, a, sa, table, *pay = call(
        functools.partial(start_kernel, seq_size),
        [low, low, ((tokens, coefs), BF16), vec, vec, ((TABLE_ROWS, channels), F32)]
        + [((states, channels + 128), BF16)] * others,
        [
            section_inputs,
            cotangent,
            w_in,
            w_bc,
            w_out,
            decay_rates,
            resets.reshape(1, tokens),
        ],
        space=pltpu.HBM,
        scratch=[
            pltpu.VMEM((tokens, width), BF16),
            pltpu.VMEM((tokens, width), BF16),
            pltpu.VMEM((width, channels), BF16),
            pltpu.VMEM((coefs, width), BF16),
            pltpu.VMEM((channels, width), BF16),
            pltpu.SMEM((1, heads), F32),
            pltpu.VMEM((1, tokens), jnp.int32),
            pltpu.SemaphoreType.DMA((5,)),
            pltpu.SemaphoreType.DMA((OUT_CHUNKS + IN_CHUNKS,)),
        ],
        flops=2 * big,
        bytes_accessed=4 * width * channels,
        name="start",
    )
    recv = [partner(pay[k - 1], "seq", k) for k in range(1, seq_size)]

    def local(gradient):
        return call(
            local_kernel,
            [vec, few, row],
            [up, gradient, coef],
            flops=big,
            bytes_accessed=4 * tokens * channels,
            name="local",
        )

    gu, gcoef, lag = local(gmp)
    state = ((states, channels), F32)
    half = width // 2
    halves = [((tokens, half), F32), ((tokens, half), BF16)]
    keep, send, adj, hpp, weight = call(
        functools.partial(first_kernel, seq_size),
        [*halves, state, state, ((others, channels), F32)],
        [up, gmp, coef, table, sa, w_in, w_bc, gu, gcoef, cotangent, *recv[::-1]],
        flops=big,
        bytes_accessed=2 * width * channels,
        name="first",
    )
    (red,) = call(
        first_parameter_kernel,
        [reduced],
        [up, gmp, coef, table, section_inputs, gu, gcoef, lag, hpp, adj],
        flops=big // 4,
        bytes_accessed=4 * tokens * channels,
        name="first_parameters",
    )
    section = lax.axis_index("section")
    kept, kept_red = None, red
    for moment in range(1, sections):
        result = (keep + swap(send, "mp").astype(F32)).astype(BF16)
        if kept is None:
            kept = result
        else:
            was_active = section == sections - moment
            kept = jnp.where(was_active, result, kept)
            kept_red = jnp.where(was_active, red, kept_red)
        mine = rotate(result, "section", -1)
        other = swap(mine, "mp")
        gmp, adjoint = call(
            hop_kernel,
            [low, ((states, channels), BF16)],
            [w_out, coef, a, table, mine, other],
            flops=big,
            bytes_accessed=2 * width * channels,
            name="hop",
        )
        recv = [partner(adjoint, "seq", k) for k in range(1, seq_size)]
        gu, gcoef, lag = local(gmp)
        last = moment == sections - 1
        rows, gcoef, *red = call(
            functools.partial(parameter_kernel, last, seq_size),
            [((coefs, channels), BF16), ((tokens, coefs), BF16)]
            + ([((coefs + 8, half), F32), ((coefs, half), BF16)] if last else [reduced]),
            [up, gmp, coef, table, section_inputs, gu, gcoef, lag, hpp, weight, kept_red, *recv],
            flops=big // 4,
            bytes_accessed=4 * tokens * channels,
            name="parameters",
        )
        if not last:
            (red,) = red
            keep, send = call(
                middle_input_kernel,
                halves,
                [rows, gu, gcoef, coef, sa, w_in, w_bc, mine, other],
                flops=big,
                bytes_accessed=2 * width * channels,
                name="middle_input",
            )
    (red,) = call(
        pair_kernel, [((coefs + 8, half), BF16)], [red[0], swap(red[1], "mp")], name="pair"
    )
    rows, red = lax.optimization_barrier((rows, red))
    (part,) = call(
        last_input_kernel,
        [low],
        [rows, gu, gcoef, coef, sa, w_in, w_bc, kept],
        flops=big,
        bytes_accessed=2 * width * channels,
        name="last_input",
    )
    (out,) = call(
        output_kernel,
        [((1, tokens, width), BF16)],
        [part, swap(part, "mp"), mine, other],
        name="output",
    )
    pieces = [partner(red, "seq", k) for k in range(1, seq_size)]
    red, out = lax.optimization_barrier((red, out))
    grad_w, grad_rates = call(
        functools.partial(total_kernel, seq_size),
        [((coefs, half), F32), ((1, heads), F32)],
        [red, *pieces],
        name="total",
    )
    (grad_w,) = call(
        join_kernel, [((1, coefs, width), F32)], [grad_w, swap(grad_w, "mp")], name="join"
    )
    return out, jnp.swapaxes(grad_w, 1, 2), grad_rates


def solution(mesh):
    return jax.shard_map(
        shards,
        mesh=mesh,
        in_specs=(
            P("section", ("groups", "seq"), None),
            P(("groups", "seq"), None),
            P("section", None, "mp"),
            P("section", None, None),
            P("section", "mp", None),
            P("section", "mp"),
            P(("groups", "seq")),
        ),
        out_specs=(
            P("section", ("groups", "seq"), None),
            P("section", "groups", None),
            P("section", ("groups", "mp")),
        ),
        check_vma=False,
    )
```

```python
import functools
import math

import jax
import jax.numpy as jnp
from jax import lax
from jax.experimental import pallas as pl
from jax.experimental.pallas import tpu as pltpu
from jax.sharding import PartitionSpec as P

LOG_KEEP = math.log(0.6)
F32 = jnp.float32
BF16 = jnp.bfloat16

NN = (((1,), (0,)), ((), ()))
NT = (((1,), (1,)), ((), ()))
TN = (((0,), (0,)), ((), ()))

RATE, EMID, ATOT, INV, COUNT = 0, 1, 2, 3, 4
TABLE_ROWS = 8
ORDERS = (
    lambda n: range(n - 1, 0, -1),
    lambda n: (1, *range(n - 1, 1, -1)),
    lambda n: (1, *range(n - 1, 1, -1)),
)
OUT_CHUNKS, IN_CHUNKS = 1, 1


def mm(a, b, dims):
    return lax.dot_general(a, b, dims, preferred_element_type=F32)


def rotate(value, axis, by):
    n = lax.axis_size(axis)
    return lax.ppermute(value, axis, [(i, (i + by) % n) for i in range(n)])


def partner(value, axis, k):
    n = lax.axis_size(axis)
    return lax.ppermute(value, axis, [(i, i ^ k) for i in range(n)])


def swap(value, axis):
    return rotate(value, axis, 1)


def expm1_small(y):
    return y * (1 + y / 2 * (1 + y / 3 * (1 + y / 4 * (1 + y / 5 * (1 + y / 6)))))


def column(tokens):
    return lax.broadcasted_iota(jnp.int32, (tokens, 1), 0).astype(F32)


def tril_mask(tokens):
    t = lax.broadcasted_iota(jnp.int32, (tokens, tokens), 0)
    s = lax.broadcasted_iota(jnp.int32, (tokens, tokens), 1)
    return t, s


def call(kernel, outs, args, *, space=pltpu.VMEM, scratch=(), flops=0, bytes_accessed=0, name=None):
    if space is pltpu.HBM:
        args = [pltpu.with_memory_space_constraint(a, space) for a in args]
    return pl.pallas_call(
        kernel,
        out_shape=[jax.ShapeDtypeStruct(s, d) for s, d in outs],
        in_specs=[pl.BlockSpec(memory_space=space) for _ in args],
        out_specs=[pl.BlockSpec(memory_space=pltpu.VMEM) for _ in outs],
        scratch_shapes=list(scratch),
        compiler_params=pltpu.CompilerParams(vmem_limit_bytes=24 << 20),
        cost_estimate=pl.CostEstimate(
            flops=flops, bytes_accessed=bytes_accessed, transcendentals=0
        ),
        name=name,
    )(*args)


def start_kernel(
    seq_size,
    x_hbm,
    g_hbm,
    w_in_hbm,
    w_bc_hbm,
    w_out_hbm,
    rates_hbm,
    resets_hbm,
    up_ref,
    gmp_ref,
    coef_ref,
    a_ref,
    sa_ref,
    table_ref,
    *refs,
):
    pay_refs = refs[: seq_size - 1]
    x_ref, g_ref, w_in_ref, w_bc_ref, w_out_ref, rates_ref, resets_ref, small_sem, wide_sem = refs[
        seq_size - 1 :
    ]
    tokens = x_hbm.shape[1]
    channels = w_in_hbm.shape[2]
    heads = rates_hbm.shape[1]
    width = channels // heads
    states = w_bc_hbm.shape[1] // 2
    small = [
        pltpu.make_async_copy(src, dst, small_sem.at[i])
        for i, (src, dst) in enumerate(
            [
                (rates_hbm, rates_ref),
                (resets_hbm, resets_ref),
                (g_hbm, g_ref),
                (x_hbm.at[0], x_ref),
                (w_bc_hbm.at[0], w_bc_ref),
            ]
        )
    ]
    rows, cols = channels // OUT_CHUNKS, channels // IN_CHUNKS
    out_parts = [slice(c * rows, (c + 1) * rows) for c in range(OUT_CHUNKS)]
    in_parts = [slice(c * cols, (c + 1) * cols) for c in range(IN_CHUNKS)]
    from_out = [
        pltpu.make_async_copy(w_out_hbm.at[0, p, :], w_out_ref.at[p, :], wide_sem.at[i])
        for i, p in enumerate(out_parts)
    ]
    from_in = [
        pltpu.make_async_copy(w_in_hbm.at[0, :, p], w_in_ref.at[:, p], wide_sem.at[OUT_CHUNKS + i])
        for i, p in enumerate(in_parts)
    ]
    for copy in small[:3] + from_out + small[3:] + from_in:
        copy.start()
    small[0].wait()
    small[1].wait()

    lane_head = lax.broadcasted_iota(jnp.int32, (1, channels), 1) // width
    rate = jnp.zeros((1, channels), F32)
    for k in range(heads):
        rate = jnp.where(lane_head == k, rates_ref[0, k], rate)
    t, s = tril_mask(tokens)
    resets = resets_ref[...].astype(F32)
    count = jnp.sum(jnp.where(s <= t, resets, 0.0), axis=1, keepdims=True)
    log = count * LOG_KEEP - (column(tokens) + 1.0) * rate
    mid = log[tokens // 2 - 1 : tokens // 2, :]
    a = jnp.exp(log - mid)
    growth = expm1_small(2.0 * rate)
    scale = jnp.sqrt(growth / (1.0 + growth))
    emid = jnp.exp(mid)
    atot = a[tokens - 1 : tokens, :]
    a_ref[...] = a
    total = jnp.broadcast_to(count[tokens - 1 : tokens, :], (1, channels))
    table_ref[...] = jnp.concatenate(
        [rate, emid, atot, 1.0 / growth, total, jnp.zeros((TABLE_ROWS - 5, channels), F32)], axis=0
    )

    small[2].wait()
    g = g_ref[...]
    for copy, part in zip(from_out, out_parts):
        copy.wait()
        gmp_ref[:, part] = (mm(g, w_out_ref[part, :], NT) * a[:, part]).astype(BF16)
    small[3].wait()
    small[4].wait()
    x = x_ref[...]
    coef = mm(x, w_bc_ref[...], NT).astype(BF16)
    coef_ref[...] = coef
    adjoint = emid * mm(coef, gmp_ref[...], TN)[states:, :]
    sa = scale / a
    sa_ref[...] = sa
    state = []
    for copy, part in zip(from_in, in_parts):
        copy.wait()
        inner = mm(x, w_in_ref[:, part], NN)
        up = (inner.astype(BF16).astype(F32) * sa[:, part]).astype(BF16)
        up_ref[:, part] = up
        state.append(atot[:, part] * mm(coef, up, TN)[:states, :])
    state = jnp.concatenate(state, axis=1)
    me = lax.axis_index("seq")
    tail = jnp.broadcast_to(count[tokens - 1 : tokens, :], (states, 128)).astype(BF16)
    for k in range(1, seq_size):
        forward = (me ^ k) > me
        pay_refs[k - 1][:, :channels] = jnp.where(forward, state, adjoint).astype(BF16)
        pay_refs[k - 1][:, channels:] = tail


def split(value):
    half = value.shape[1] // 2
    low = lax.axis_index("mp") == 0
    left, right = value[:, :half], value[:, half:]
    return jnp.where(low, left, right), jnp.where(low, right, left)


def joined(mine, other):
    low = lax.axis_index("mp") == 0
    return jnp.concatenate([jnp.where(low, mine, other), jnp.where(low, other, mine)], axis=1)


def coef_grads(gs, b_part, c_part):
    return jnp.concatenate([mm(gs, c_part, TN), mm(gs, b_part, NN)], axis=1)


def local_kernel(up_ref, gmp_ref, coef_ref, gu_ref, gcoef_ref, lag_ref):
    tokens = up_ref.shape[0]
    states = coef_ref.shape[1] // 2
    up, gmp = up_ref[...], gmp_ref[...]
    coef = coef_ref[...]
    b_part, c_part = coef[:, :states], coef[:, states:]
    t, s = tril_mask(tokens)
    causal = s <= t
    scores = jnp.where(causal, mm(c_part, b_part, NT), 0.0)
    gu_ref[...] = mm(scores.astype(BF16), gmp, TN)
    lagged = (scores * (t - s).astype(F32)).astype(BF16)
    lag_ref[...] = jnp.sum(gmp.astype(F32) * mm(lagged, up, NN), axis=0, keepdims=True)
    gs = jnp.where(causal, mm(gmp, up, NT), 0.0).astype(BF16)
    gcoef_ref[...] = coef_grads(gs, b_part, c_part)


def unpack(seq_size, recv_refs, table_ref, states, tokens):
    channels = table_ref.shape[1]
    rate = table_ref[RATE : RATE + 1, :]
    me = lax.axis_index("seq")
    source = [me ^ k for k in ORDERS[0](seq_size)]
    data = [r[:, :channels].astype(F32) for r in recv_refs]
    gap = [
        r[:1, channels : channels + 1].astype(F32) * LOG_KEEP - tokens * rate for r in recv_refs
    ]
    h_in = jnp.zeros((states, channels), F32)
    adj = jnp.zeros((states, channels), F32)
    weights = []
    for i, src in enumerate(source):
        forward = src < me
        low, high = jnp.minimum(src, me), jnp.maximum(src, me)
        log = jnp.zeros((1, channels), F32)
        for j, other in enumerate(source):
            if j != i:
                between = jnp.logical_and(other > low, other < high)
                log = log + jnp.where(between, gap[j], 0.0)
        weight = jnp.exp(log)
        term = weight * data[i]
        h_in = h_in + jnp.where(forward, term, 0.0)
        adj = adj + jnp.where(forward, 0.0, term)
        weights.append(jnp.where(forward, 0.0, weight))
    return h_in, adj, weights


def state_rows(hpp):
    return jnp.concatenate([jnp.zeros_like(hpp), hpp], axis=0).astype(BF16)


def input_gradient(rows, gu, gcoef, coef, sa_ref, w_in_ref, w_bc_ref):
    grad_inner = (sa_ref[...] * (gu + mm(coef, rows, NN))).astype(BF16)
    return mm(grad_inner, w_in_ref[0], NT) + mm(gcoef, w_bc_ref[0], NN)


def adjoint_rows(adj, table_ref):
    adjp = table_ref[ATOT : ATOT + 1, :] * adj
    return jnp.concatenate([adjp, jnp.zeros_like(adjp)], axis=0).astype(BF16)


def coef_total(rows, h_rows, gcoef_ref, up, gmp):
    return (gcoef_ref[...] + mm(gmp, h_rows, NT) + mm(up, rows, NT)).astype(BF16)


def rate_gradients(adj, hpp, gu_ref, lag_ref, up_ref, gmp_ref, coef_ref, table_ref):
    tokens = up_ref.shape[0]
    coef = coef_ref[...]
    adjp = table_ref[ATOT : ATOT + 1, :] * adj
    v = mm(coef, adjoint_rows(adj, table_ref), NN)
    ch = mm(coef, state_rows(hpp), NN)
    place = column(tokens)
    up_f, gmp_f = up_ref[...].astype(F32), gmp_ref[...].astype(F32)
    lag = (
        lag_ref[...]
        + jnp.sum(gmp_f * ((place + 1.0) * ch), axis=0, keepdims=True)
        + jnp.sum(up_f * ((tokens - 1.0 - place) * v), axis=0, keepdims=True)
        + tokens * jnp.sum(hpp * adjp, axis=0, keepdims=True)
    )
    total = jnp.sum(up_f * (gu_ref[...] + v), axis=0, keepdims=True)
    return total * table_ref[INV : INV + 1, :] - lag


def first_kernel(
    seq_size,
    up_ref,
    gmp_ref,
    coef_ref,
    table_ref,
    sa_ref,
    w_in_ref,
    w_bc_ref,
    gu_ref,
    gcoef_ref,
    g_ref,
    *refs,
):
    recv_refs, (keep_ref, send_ref, adj_ref, hpp_ref, weight_ref) = (
        refs[: seq_size - 1],
        refs[seq_size - 1 :],
    )
    tokens = up_ref.shape[0]
    states = coef_ref.shape[1] // 2
    h_in, adj, weights = unpack(seq_size, recv_refs, table_ref, states, tokens)
    hpp = table_ref[EMID : EMID + 1, :] * h_in
    hpp_ref[...] = hpp
    for k, weight in zip(ORDERS[0](seq_size), weights):
        weight_ref[k - 1 : k, :] = weight
    adj_ref[...] = adj
    rows = adjoint_rows(adj, table_ref)
    gcoef = coef_total(rows, state_rows(hpp), gcoef_ref, up_ref[...], gmp_ref[...])
    back = input_gradient(rows, gu_ref[...], gcoef, coef_ref[...], sa_ref, w_in_ref, w_bc_ref)
    store_split(back, g_ref[...], keep_ref, send_ref)


def store_split(back, g, keep_ref, send_ref):
    keep, send = split(back)
    keep_ref[...] = keep + split(g)[0].astype(F32)
    send_ref[...] = send.astype(BF16)


def gather_adjoint(recv_refs, weight_ref):
    adj = None
    for k, r in zip(ORDERS[1](len(recv_refs) + 1), recv_refs):
        term = weight_ref[k - 1 : k, :] * r[...].astype(F32)
        adj = term if adj is None else adj + term
    return adj


def first_parameter_kernel(
    up_ref,
    gmp_ref,
    coef_ref,
    table_ref,
    x_ref,
    gu_ref,
    gcoef_ref,
    lag_ref,
    hpp_ref,
    adj_ref,
    dw_ref,
    rate_ref,
):
    adj, hpp = adj_ref[...], hpp_ref[...]
    gcoef = coef_total(
        adjoint_rows(adj, table_ref), state_rows(hpp), gcoef_ref, up_ref[...], gmp_ref[...]
    )
    dw_ref[...] = mm(gcoef, x_ref[0], TN)
    rate_ref[...] = rate_gradients(
        adj, hpp, gu_ref, lag_ref, up_ref, gmp_ref, coef_ref, table_ref
    )


def parameter_kernel(
    last,
    seq_size,
    up_ref,
    gmp_ref,
    table_ref,
    x_ref,
    gcoef_in_ref,
    hpp_ref,
    weight_ref,
    kept_ref,
    *refs,
):
    recv_refs, (adj_ref, rows_ref, gcoef_ref, *out_refs) = refs[: seq_size - 1], refs[seq_size - 1 :]
    adj = gather_adjoint(recv_refs, weight_ref)
    adj_ref[...] = adj
    rows = adjoint_rows(adj, table_ref)
    rows_ref[...] = rows
    gcoef = coef_total(rows, state_rows(hpp_ref[...]), gcoef_in_ref, up_ref[...], gmp_ref[...])
    gcoef_ref[...] = gcoef
    dw = mm(gcoef, x_ref[0], TN)
    if not last:
        out_refs[0][...] = dw
        return
    keep_ref, send_ref = out_refs
    keep_ref[...], send = split(jnp.where(lax.axis_index("section") == 0, dw, kept_ref[...]))
    send_ref[...] = send.astype(BF16)


def rate_kernel(
    last,
    up_ref,
    gmp_ref,
    coef_ref,
    table_ref,
    gu_ref,
    lag_ref,
    hpp_ref,
    adj_ref,
    kept_ref,
    rate_ref,
):
    rate = rate_gradients(
        adj_ref[...], hpp_ref[...], gu_ref, lag_ref, up_ref, gmp_ref, coef_ref, table_ref
    )
    if last:
        rate = jnp.where(lax.axis_index("section") == 0, rate, kept_ref[...])
    rate_ref[...] = rate


def middle_input_kernel(
    rows_ref, gu_ref, gcoef_ref, coef_ref, sa_ref, w_in_ref, w_bc_ref, mine_ref, other_ref, keep_ref, send_ref
):
    back = input_gradient(
        rows_ref[...], gu_ref[...], gcoef_ref[...], coef_ref[...], sa_ref, w_in_ref, w_bc_ref
    )
    store_split(back, joined(mine_ref[...], other_ref[...]), keep_ref, send_ref)


def last_input_kernel(
    rows_ref, gu_ref, gcoef_ref, coef_ref, sa_ref, w_in_ref, w_bc_ref, kept_ref, part_ref
):
    back = input_gradient(
        rows_ref[...], gu_ref[...], gcoef_ref[...], coef_ref[...], sa_ref, w_in_ref, w_bc_ref
    )
    half = kept_ref[...]
    zero = jnp.zeros_like(half)
    low = lax.axis_index("mp") == 0
    done = jnp.concatenate([jnp.where(low, half, zero), jnp.where(low, zero, half)], axis=1)
    part_ref[...] = jnp.where(lax.axis_index("section") == 0, back.astype(BF16), done)


def scaled_gradient(g, w_out_ref, coef, a_ref, table_ref):
    gmp = (a_ref[...] * mm(g, w_out_ref[0], NT)).astype(BF16)
    states = coef.shape[1] // 2
    adjoint = table_ref[EMID : EMID + 1, :] * mm(coef, gmp, TN)[states:, :]
    return gmp, adjoint


def hop_kernel(
    w_out_ref, coef_ref, a_ref, table_ref, mine_ref, other_ref, gmp_ref, adjoint_ref
):
    g = joined(mine_ref[...], other_ref[...])
    gmp, adjoint = scaled_gradient(g, w_out_ref, coef_ref[...], a_ref, table_ref)
    gmp_ref[...] = gmp
    adjoint_ref[...] = adjoint.astype(BF16)


def pair_kernel(keep_ref, other_ref, rate_ref, sum_ref):
    coefs, half = keep_ref.shape
    sum_ref[:coefs, :] = (keep_ref[...] + other_ref[...].astype(F32)).astype(BF16)
    rate = jnp.concatenate([rate_ref[:, :half], rate_ref[:, half:], jnp.zeros((6, half), F32)], axis=0)
    sum_ref[coefs:, :] = rate.astype(BF16)


def total_kernel(seq_size, *refs):
    pieces, (w_ref, rate_ref) = refs[:seq_size], refs[seq_size:]
    ranges = [0, *ORDERS[2](seq_size)]
    terms = [pieces[ranges.index(k)][...].astype(F32) for k in range(seq_size)]
    while len(terms) > 1:
        terms = [x + y for x, y in zip(terms[::2], terms[1::2])]
    total = terms[0]
    coefs = w_ref.shape[0]
    w_ref[...] = total[:coefs, :]
    rate_ref[...] = total[coefs:, :]


def head_kernel(row_ref, rate_ref):
    heads, channels = rate_ref.shape[1], 2 * row_ref.shape[1]
    row = jnp.concatenate([row_ref[:1, :], row_ref[1:2, :]], axis=1)
    lane = lax.broadcasted_iota(jnp.int32, (heads, channels), 1) // (channels // heads)
    head = lax.broadcasted_iota(jnp.int32, (heads, channels), 0)
    col = jnp.sum(jnp.where(lane == head, row, 0.0), axis=1, keepdims=True)
    i = lax.broadcasted_iota(jnp.int32, (heads, heads), 0)
    j = lax.broadcasted_iota(jnp.int32, (heads, heads), 1)
    rate_ref[...] = jnp.sum(jnp.where(i == j, col, 0.0), axis=0, keepdims=True)


def output_kernel(part_ref, part2_ref, mine_ref, other_ref, out_ref):
    active = lax.axis_index("section") == 0
    g = jnp.where(active, joined(mine_ref[...], other_ref[...]).astype(F32), 0.0)
    out_ref[0] = (g + (part_ref[...].astype(F32) + part2_ref[...].astype(F32))).astype(BF16)


def join_kernel(mine_ref, other_ref, out_ref):
    out_ref[0] = joined(mine_ref[...], other_ref[...])


def shards(section_inputs, cotangent, w_in, w_bc, w_out, decay_rates, resets):
    tokens, width = cotangent.shape
    channels = w_in.shape[2]
    coefs = w_bc.shape[2]
    w_bc = jnp.swapaxes(w_bc, 1, 2)
    states = coefs // 2
    heads = decay_rates.shape[1]
    seq_size = lax.axis_size("seq")
    sections = lax.axis_size("section")
    others = seq_size - 1
    big = 2 * tokens * width * channels
    vec, low = ((tokens, channels), F32), ((tokens, channels), BF16)
    row = ((1, channels), F32)
    few = ((tokens, coefs), F32)
    wide = ((coefs, width), F32)

    up, gmp, coef, a, sa, table, *pay = call(
        functools.partial(start_kernel, seq_size),
        [low, low, ((tokens, coefs), BF16), vec, vec, ((TABLE_ROWS, channels), F32)]
        + [((states, channels + 128), BF16)] * others,
        [
            section_inputs,
            cotangent,
            w_in,
            w_bc,
            w_out,
            decay_rates,
            resets.reshape(1, tokens),
        ],
        space=pltpu.HBM,
        scratch=[
            pltpu.VMEM((tokens, width), BF16),
            pltpu.VMEM((tokens, width), BF16),
            pltpu.VMEM((width, channels), BF16),
            pltpu.VMEM((coefs, width), BF16),
            pltpu.VMEM((channels, width), BF16),
            pltpu.SMEM((1, heads), F32),
            pltpu.VMEM((1, tokens), jnp.int32),
            pltpu.SemaphoreType.DMA((5,)),
            pltpu.SemaphoreType.DMA((OUT_CHUNKS + IN_CHUNKS,)),
        ],
        flops=2 * big,
        bytes_accessed=4 * width * channels,
        name="start",
    )
    recv = [partner(pay[k - 1], "seq", k) for k in ORDERS[0](seq_size)]

    def local(gradient):
        return call(
            local_kernel,
            [vec, few, row],
            [up, gradient, coef],
            flops=big,
            bytes_accessed=4 * tokens * channels,
            name="local",
        )

    gu, gcoef, lag = local(gmp)
    state = ((states, channels), F32)
    half = width // 2
    halves = [((tokens, half), F32), ((tokens, half), BF16)]
    keep, send, adj, hpp, weight = call(
        functools.partial(first_kernel, seq_size),
        [*halves, state, state, ((others, channels), F32)],
        [up, gmp, coef, table, sa, w_in, w_bc, gu, gcoef, cotangent, *recv],
        flops=big,
        bytes_accessed=2 * width * channels,
        name="first",
    )
    dw, rate = call(
        first_parameter_kernel,
        [wide, row],
        [up, gmp, coef, table, section_inputs, gu, gcoef, lag, hpp, adj],
        flops=big // 4,
        bytes_accessed=4 * tokens * channels,
        name="first_parameters",
    )
    section = lax.axis_index("section")
    kept, kept_dw, kept_rate = None, dw, rate
    for moment in range(1, sections):
        result = (keep + swap(send, "mp").astype(F32)).astype(BF16)
        if kept is None:
            kept = result
        else:
            was_active = section == sections - moment
            kept = jnp.where(was_active, result, kept)
            kept_dw = jnp.where(was_active, dw, kept_dw)
            kept_rate = jnp.where(was_active, rate, kept_rate)
        mine = rotate(result, "section", -1)
        if moment == 1:
            mine, kept_dw, kept_rate = lax.optimization_barrier((mine, kept_dw, kept_rate))
        other = swap(mine, "mp")
        gmp, adjoint = call(
            hop_kernel,
            [low, ((states, channels), BF16)],
            [w_out, coef, a, table, mine, other],
            flops=big,
            bytes_accessed=2 * width * channels,
            name="hop",
        )
        recv = [partner(adjoint, "seq", k) for k in ORDERS[1](seq_size)]
        gu, gcoef, lag = local(gmp)
        last = moment == sections - 1
        adj, rows, gcoef, *dw = call(
            functools.partial(parameter_kernel, last, seq_size),
            [state, ((coefs, channels), BF16), ((tokens, coefs), BF16)]
            + ([((coefs, half), F32), ((coefs, half), BF16)] if last else [wide]),
            [up, gmp, table, section_inputs, gcoef, hpp, weight, kept_dw, *recv],
            flops=big // 4,
            bytes_accessed=4 * tokens * channels,
            name="parameters",
        )
        (rate,) = call(
            functools.partial(rate_kernel, last),
            [row],
            [up, gmp, coef, table, gu, lag, hpp, adj, kept_rate],
            flops=big // 8,
            bytes_accessed=4 * tokens * channels,
            name="rates",
        )
        if not last:
            (dw,) = dw
            keep, send = call(
                middle_input_kernel,
                halves,
                [rows, gu, gcoef, coef, sa, w_in, w_bc, mine, other],
                flops=big,
                bytes_accessed=2 * width * channels,
                name="middle_input",
            )
    (red,) = call(
        pair_kernel, [((coefs + 8, half), BF16)], [dw[0], swap(dw[1], "mp"), rate], name="pair"
    )
    (part,) = call(
        last_input_kernel,
        [low],
        [rows, gu, gcoef, coef, sa, w_in, w_bc, kept],
        flops=big,
        bytes_accessed=2 * width * channels,
        name="last_input",
    )
    part, red = lax.optimization_barrier((part, red))
    (out,) = call(
        output_kernel,
        [((1, tokens, width), BF16)],
        [part, swap(part, "mp"), mine, other],
        name="output",
    )
    pieces = [partner(red, "seq", k) for k in ORDERS[2](seq_size)]
    red, out = lax.optimization_barrier((red, out))
    grad_w, rate = call(
        functools.partial(total_kernel, seq_size),
        [((coefs, half), F32), ((8, half), F32)],
        [red, *pieces],
        name="total",
    )
    (grad_rates,) = call(head_kernel, [((1, heads), F32)], [rate], name="heads")
    (grad_w,) = call(
        join_kernel, [((1, coefs, width), F32)], [grad_w, swap(grad_w, "mp")], name="join"
    )
    return out, jnp.swapaxes(grad_w, 1, 2), grad_rates


def solution(mesh):
    return jax.shard_map(
        shards,
        mesh=mesh,
        in_specs=(
            P("section", ("groups", "seq"), None),
            P(("groups", "seq"), None),
            P("section", None, "mp"),
            P("section", None, None),
            P("section", "mp", None),
            P("section", "mp"),
            P(("groups", "seq")),
        ),
        out_specs=(
            P("section", ("groups", "seq"), None),
            P("section", "groups", None),
            P("section", ("groups", "mp")),
        ),
        check_vma=False,
    )
```

```python
import functools
import math

import jax
import jax.numpy as jnp
from jax import lax
from jax.experimental import pallas as pl
from jax.experimental.pallas import tpu as pltpu
from jax.sharding import PartitionSpec as P

LOG_KEEP = math.log(0.6)
F32 = jnp.float32
BF16 = jnp.bfloat16

NN = (((1,), (0,)), ((), ()))
NT = (((1,), (1,)), ((), ()))
TN = (((0,), (0,)), ((), ()))

RATE, EMID, ATOT, INV, COUNT = 0, 1, 2, 3, 4
TABLE_ROWS = 8
ORDERS = (lambda n: range(n - 1, 0, -1), lambda n: range(1, n), lambda n: range(1, n))
OUT_CHUNKS, IN_CHUNKS = 1, 1


def mm(a, b, dims):
    return lax.dot_general(a, b, dims, preferred_element_type=F32)


def rotate(value, axis, by):
    n = lax.axis_size(axis)
    return lax.ppermute(value, axis, [(i, (i + by) % n) for i in range(n)])


def partner(value, axis, k):
    n = lax.axis_size(axis)
    return lax.ppermute(value, axis, [(i, i ^ k) for i in range(n)])


def swap(value, axis):
    return rotate(value, axis, 1)


def expm1_small(y):
    return y * (1 + y / 2 * (1 + y / 3 * (1 + y / 4 * (1 + y / 5 * (1 + y / 6)))))


def column(tokens):
    return lax.broadcasted_iota(jnp.int32, (tokens, 1), 0).astype(F32)


def tril_mask(tokens):
    t = lax.broadcasted_iota(jnp.int32, (tokens, tokens), 0)
    s = lax.broadcasted_iota(jnp.int32, (tokens, tokens), 1)
    return t, s


def call(kernel, outs, args, *, space=pltpu.VMEM, scratch=(), flops=0, bytes_accessed=0, name=None):
    if space is pltpu.HBM:
        args = [pltpu.with_memory_space_constraint(a, space) for a in args]
    return pl.pallas_call(
        kernel,
        out_shape=[jax.ShapeDtypeStruct(s, d) for s, d in outs],
        in_specs=[pl.BlockSpec(memory_space=space) for _ in args],
        out_specs=[pl.BlockSpec(memory_space=pltpu.VMEM) for _ in outs],
        scratch_shapes=list(scratch),
        compiler_params=pltpu.CompilerParams(vmem_limit_bytes=24 << 20),
        cost_estimate=pl.CostEstimate(
            flops=flops, bytes_accessed=bytes_accessed, transcendentals=0
        ),
        name=name,
    )(*args)


def start_kernel(
    seq_size,
    x_hbm,
    g_hbm,
    w_in_hbm,
    w_bc_hbm,
    w_out_hbm,
    rates_hbm,
    resets_hbm,
    up_ref,
    gmp_ref,
    coef_ref,
    a_ref,
    sa_ref,
    table_ref,
    *refs,
):
    pay_refs = refs[: seq_size - 1]
    x_ref, g_ref, w_in_ref, w_bc_ref, w_out_ref, rates_ref, resets_ref, small_sem, wide_sem = refs[
        seq_size - 1 :
    ]
    tokens = x_hbm.shape[1]
    channels = w_in_hbm.shape[2]
    heads = rates_hbm.shape[1]
    width = channels // heads
    states = w_bc_hbm.shape[1] // 2
    small = [
        pltpu.make_async_copy(src, dst, small_sem.at[i])
        for i, (src, dst) in enumerate(
            [
                (rates_hbm, rates_ref),
                (resets_hbm, resets_ref),
                (g_hbm, g_ref),
                (x_hbm.at[0], x_ref),
                (w_bc_hbm.at[0], w_bc_ref),
            ]
        )
    ]
    rows, cols = channels // OUT_CHUNKS, channels // IN_CHUNKS
    out_parts = [slice(c * rows, (c + 1) * rows) for c in range(OUT_CHUNKS)]
    in_parts = [slice(c * cols, (c + 1) * cols) for c in range(IN_CHUNKS)]
    from_out = [
        pltpu.make_async_copy(w_out_hbm.at[0, p, :], w_out_ref.at[p, :], wide_sem.at[i])
        for i, p in enumerate(out_parts)
    ]
    from_in = [
        pltpu.make_async_copy(w_in_hbm.at[0, :, p], w_in_ref.at[:, p], wide_sem.at[OUT_CHUNKS + i])
        for i, p in enumerate(in_parts)
    ]
    for copy in small[:3] + from_out + small[3:] + from_in:
        copy.start()
    small[0].wait()
    small[1].wait()

    lane_head = lax.broadcasted_iota(jnp.int32, (1, channels), 1) // width
    rate = jnp.zeros((1, channels), F32)
    for k in range(heads):
        rate = jnp.where(lane_head == k, rates_ref[0, k], rate)
    t, s = tril_mask(tokens)
    resets = resets_ref[...].astype(F32)
    count = jnp.sum(jnp.where(s <= t, resets, 0.0), axis=1, keepdims=True)
    log = count * LOG_KEEP - (column(tokens) + 1.0) * rate
    mid = log[tokens // 2 - 1 : tokens // 2, :]
    a = jnp.exp(log - mid)
    growth = expm1_small(2.0 * rate)
    scale = jnp.sqrt(growth / (1.0 + growth))
    emid = jnp.exp(mid)
    atot = a[tokens - 1 : tokens, :]
    a_ref[...] = a
    total = jnp.broadcast_to(count[tokens - 1 : tokens, :], (1, channels))
    table_ref[...] = jnp.concatenate(
        [rate, emid, atot, 1.0 / growth, total, jnp.zeros((TABLE_ROWS - 5, channels), F32)], axis=0
    )

    small[2].wait()
    g = g_ref[...]
    for copy, part in zip(from_out, out_parts):
        copy.wait()
        gmp_ref[:, part] = (mm(g, w_out_ref[part, :], NT) * a[:, part]).astype(BF16)
    small[3].wait()
    small[4].wait()
    x = x_ref[...]
    coef = mm(x, w_bc_ref[...], NT).astype(BF16)
    coef_ref[...] = coef
    adjoint = emid * mm(coef, gmp_ref[...], TN)[states:, :]
    sa = scale / a
    sa_ref[...] = sa
    state = []
    for copy, part in zip(from_in, in_parts):
        copy.wait()
        inner = mm(x, w_in_ref[:, part], NN)
        up = (inner.astype(BF16).astype(F32) * sa[:, part]).astype(BF16)
        up_ref[:, part] = up
        state.append(atot[:, part] * mm(coef, up, TN)[:states, :])
    state = jnp.concatenate(state, axis=1)
    me = lax.axis_index("seq")
    tail = jnp.broadcast_to(count[tokens - 1 : tokens, :], (states, 128)).astype(BF16)
    for k in range(1, seq_size):
        forward = (me ^ k) > me
        pay_refs[k - 1][:, :channels] = jnp.where(forward, state, adjoint).astype(BF16)
        pay_refs[k - 1][:, channels:] = tail


def split(value):
    half = value.shape[1] // 2
    low = lax.axis_index("mp") == 0
    left, right = value[:, :half], value[:, half:]
    return jnp.where(low, left, right), jnp.where(low, right, left)


def joined(mine, other):
    low = lax.axis_index("mp") == 0
    return jnp.concatenate([jnp.where(low, mine, other), jnp.where(low, other, mine)], axis=1)


def turn_kernel(w_ref, after_ref, out_ref):
    out_ref[...] = w_ref[0].T


def coef_grads(gs, b_part, c_part):
    return jnp.concatenate([mm(gs, c_part, TN), mm(gs, b_part, NN)], axis=1)


def local_kernel(up_ref, gmp_ref, coef_ref, gu_ref, gcoef_ref, lag_ref):
    tokens = up_ref.shape[0]
    states = coef_ref.shape[1] // 2
    up, gmp = up_ref[...], gmp_ref[...]
    coef = coef_ref[...]
    b_part, c_part = coef[:, :states], coef[:, states:]
    t, s = tril_mask(tokens)
    causal = s <= t
    scores = jnp.where(causal, mm(c_part, b_part, NT), 0.0)
    gu_ref[...] = mm(scores.astype(BF16), gmp, TN)
    lagged = (scores * (t - s).astype(F32)).astype(BF16)
    lag_ref[...] = jnp.sum(gmp.astype(F32) * mm(lagged, up, NN), axis=0, keepdims=True)
    gs = jnp.where(causal, mm(gmp, up, NT), 0.0).astype(BF16)
    gcoef_ref[...] = coef_grads(gs, b_part, c_part)


def unpack(seq_size, recv_refs, table_ref, states, tokens):
    channels = table_ref.shape[1]
    rate = table_ref[RATE : RATE + 1, :]
    me = lax.axis_index("seq")
    source = [me ^ k for k in ORDERS[0](seq_size)]
    data = [r[:, :channels].astype(F32) for r in recv_refs]
    gap = [
        r[:1, channels : channels + 1].astype(F32) * LOG_KEEP - tokens * rate for r in recv_refs
    ]
    h_in = jnp.zeros((states, channels), F32)
    adj = jnp.zeros((states, channels), F32)
    weights = []
    for i, src in enumerate(source):
        forward = src < me
        low, high = jnp.minimum(src, me), jnp.maximum(src, me)
        log = jnp.zeros((1, channels), F32)
        for j, other in enumerate(source):
            if j != i:
                between = jnp.logical_and(other > low, other < high)
                log = log + jnp.where(between, gap[j], 0.0)
        weight = jnp.exp(log)
        term = weight * data[i]
        h_in = h_in + jnp.where(forward, term, 0.0)
        adj = adj + jnp.where(forward, 0.0, term)
        weights.append(jnp.where(forward, 0.0, weight))
    return h_in, adj, weights


def state_rows(hpp):
    return jnp.concatenate([jnp.zeros_like(hpp), hpp], axis=0).astype(BF16)


def input_gradient(rows, gu, gcoef, coef, sa_ref, w_in_ref, w_bc_ref):
    grad_inner = (sa_ref[...] * (gu + mm(coef, rows, NN))).astype(BF16)
    return mm(grad_inner, w_in_ref[...], NN) + mm(gcoef, w_bc_ref[0], NN)


def adjoint_rows(adj, table_ref):
    adjp = table_ref[ATOT : ATOT + 1, :] * adj
    return jnp.concatenate([adjp, jnp.zeros_like(adjp)], axis=0).astype(BF16)


def coef_total(rows, h_rows, gcoef_ref, up, gmp):
    return (gcoef_ref[...] + mm(gmp, h_rows, NT) + mm(up, rows, NT)).astype(BF16)


def rate_gradients(adj, hpp, gu_ref, lag_ref, up_ref, gmp_ref, coef_ref, table_ref):
    tokens = up_ref.shape[0]
    coef = coef_ref[...]
    adjp = table_ref[ATOT : ATOT + 1, :] * adj
    v = mm(coef, adjoint_rows(adj, table_ref), NN)
    ch = mm(coef, state_rows(hpp), NN)
    place = column(tokens)
    up_f, gmp_f = up_ref[...].astype(F32), gmp_ref[...].astype(F32)
    lag = (
        lag_ref[...]
        + jnp.sum(gmp_f * ((place + 1.0) * ch), axis=0, keepdims=True)
        + jnp.sum(up_f * ((tokens - 1.0 - place) * v), axis=0, keepdims=True)
        + tokens * jnp.sum(hpp * adjp, axis=0, keepdims=True)
    )
    total = jnp.sum(up_f * (gu_ref[...] + v), axis=0, keepdims=True)
    return total * table_ref[INV : INV + 1, :] - lag


def first_kernel(
    seq_size,
    up_ref,
    gmp_ref,
    coef_ref,
    table_ref,
    sa_ref,
    w_in_ref,
    w_bc_ref,
    gu_ref,
    gcoef_ref,
    g_ref,
    *refs,
):
    recv_refs, (keep_ref, send_ref, adj_ref, hpp_ref, weight_ref) = (
        refs[: seq_size - 1],
        refs[seq_size - 1 :],
    )
    tokens = up_ref.shape[0]
    states = coef_ref.shape[1] // 2
    h_in, adj, weights = unpack(seq_size, recv_refs, table_ref, states, tokens)
    hpp = table_ref[EMID : EMID + 1, :] * h_in
    hpp_ref[...] = hpp
    for k, weight in zip(ORDERS[0](seq_size), weights):
        weight_ref[k - 1 : k, :] = weight
    adj_ref[...] = adj
    rows = adjoint_rows(adj, table_ref)
    gcoef = coef_total(rows, state_rows(hpp), gcoef_ref, up_ref[...], gmp_ref[...])
    back = input_gradient(rows, gu_ref[...], gcoef, coef_ref[...], sa_ref, w_in_ref, w_bc_ref)
    store_split(back, g_ref[...], keep_ref, send_ref)


def store_split(back, g, keep_ref, send_ref):
    keep, send = split(back)
    keep_ref[...] = keep + split(g)[0].astype(F32)
    send_ref[...] = send.astype(BF16)


def gather_adjoint(recv_refs, weight_ref):
    adj = None
    for k, r in zip(ORDERS[1](len(recv_refs) + 1), recv_refs):
        term = weight_ref[k - 1 : k, :] * r[...].astype(F32)
        adj = term if adj is None else adj + term
    return adj


def first_parameter_kernel(
    up_ref,
    gmp_ref,
    coef_ref,
    table_ref,
    x_ref,
    gu_ref,
    gcoef_ref,
    lag_ref,
    hpp_ref,
    adj_ref,
    dw_ref,
    rate_ref,
):
    adj, hpp = adj_ref[...], hpp_ref[...]
    gcoef = coef_total(
        adjoint_rows(adj, table_ref), state_rows(hpp), gcoef_ref, up_ref[...], gmp_ref[...]
    )
    dw_ref[...] = mm(gcoef, x_ref[0], TN)
    rate_ref[...] = rate_gradients(
        adj, hpp, gu_ref, lag_ref, up_ref, gmp_ref, coef_ref, table_ref
    )


def parameter_kernel(
    last,
    seq_size,
    up_ref,
    gmp_ref,
    table_ref,
    x_ref,
    gcoef_in_ref,
    hpp_ref,
    weight_ref,
    kept_ref,
    *refs,
):
    recv_refs, (adj_ref, rows_ref, gcoef_ref, *out_refs) = refs[: seq_size - 1], refs[seq_size - 1 :]
    adj = gather_adjoint(recv_refs, weight_ref)
    adj_ref[...] = adj
    rows = adjoint_rows(adj, table_ref)
    rows_ref[...] = rows
    gcoef = coef_total(rows, state_rows(hpp_ref[...]), gcoef_in_ref, up_ref[...], gmp_ref[...])
    gcoef_ref[...] = gcoef
    dw = mm(gcoef, x_ref[0], TN)
    if not last:
        out_refs[0][...] = dw
        return
    keep_ref, send_ref = out_refs
    keep_ref[...], send = split(jnp.where(lax.axis_index("section") == 0, dw, kept_ref[...]))
    send_ref[...] = send.astype(BF16)


def rate_kernel(
    last,
    up_ref,
    gmp_ref,
    coef_ref,
    table_ref,
    gu_ref,
    lag_ref,
    hpp_ref,
    adj_ref,
    kept_ref,
    rate_ref,
):
    rate = rate_gradients(
        adj_ref[...], hpp_ref[...], gu_ref, lag_ref, up_ref, gmp_ref, coef_ref, table_ref
    )
    if last:
        rate = jnp.where(lax.axis_index("section") == 0, rate, kept_ref[...])
    rate_ref[...] = rate


def middle_input_kernel(
    rows_ref, gu_ref, gcoef_ref, coef_ref, sa_ref, w_in_ref, w_bc_ref, mine_ref, other_ref, keep_ref, send_ref
):
    back = input_gradient(
        rows_ref[...], gu_ref[...], gcoef_ref[...], coef_ref[...], sa_ref, w_in_ref, w_bc_ref
    )
    store_split(back, joined(mine_ref[...], other_ref[...]), keep_ref, send_ref)


def last_input_kernel(
    rows_ref, gu_ref, gcoef_ref, coef_ref, sa_ref, w_in_ref, w_bc_ref, kept_ref, part_ref
):
    back = input_gradient(
        rows_ref[...], gu_ref[...], gcoef_ref[...], coef_ref[...], sa_ref, w_in_ref, w_bc_ref
    )
    half = kept_ref[...]
    zero = jnp.zeros_like(half)
    low = lax.axis_index("mp") == 0
    done = jnp.concatenate([jnp.where(low, half, zero), jnp.where(low, zero, half)], axis=1)
    part_ref[...] = jnp.where(lax.axis_index("section") == 0, back.astype(BF16), done)


def scaled_gradient(g, w_out_ref, coef, a_ref, table_ref):
    gmp = (a_ref[...] * mm(g, w_out_ref[...], NN)).astype(BF16)
    states = coef.shape[1] // 2
    adjoint = table_ref[EMID : EMID + 1, :] * mm(coef, gmp, TN)[states:, :]
    return gmp, adjoint


def hop_kernel(
    w_out_ref, coef_ref, a_ref, table_ref, mine_ref, other_ref, gmp_ref, adjoint_ref
):
    g = joined(mine_ref[...], other_ref[...])
    gmp, adjoint = scaled_gradient(g, w_out_ref, coef_ref[...], a_ref, table_ref)
    gmp_ref[...] = gmp
    adjoint_ref[...] = adjoint.astype(BF16)


def pair_kernel(keep_ref, other_ref, rate_ref, sum_ref):
    coefs, half = keep_ref.shape
    sum_ref[:coefs, :] = (keep_ref[...] + other_ref[...].astype(F32)).astype(BF16)
    rate = jnp.concatenate([rate_ref[:, :half], rate_ref[:, half:], jnp.zeros((6, half), F32)], axis=0)
    sum_ref[coefs:, :] = rate.astype(BF16)


def total_kernel(seq_size, *refs):
    pieces, (w_ref, rate_ref) = refs[:seq_size], refs[seq_size:]
    ranges = [0, *ORDERS[2](seq_size)]
    terms = [pieces[ranges.index(k)][...].astype(F32) for k in range(seq_size)]
    while len(terms) > 1:
        terms = [x + y for x, y in zip(terms[::2], terms[1::2])]
    total = terms[0]
    coefs = w_ref.shape[0]
    w_ref[...] = total[:coefs, :]
    rate_ref[...] = total[coefs:, :]


def head_kernel(row_ref, rate_ref):
    heads, channels = rate_ref.shape[1], 2 * row_ref.shape[1]
    row = jnp.concatenate([row_ref[:1, :], row_ref[1:2, :]], axis=1)
    lane = lax.broadcasted_iota(jnp.int32, (heads, channels), 1) // (channels // heads)
    head = lax.broadcasted_iota(jnp.int32, (heads, channels), 0)
    col = jnp.sum(jnp.where(lane == head, row, 0.0), axis=1, keepdims=True)
    i = lax.broadcasted_iota(jnp.int32, (heads, heads), 0)
    j = lax.broadcasted_iota(jnp.int32, (heads, heads), 1)
    rate_ref[...] = jnp.sum(jnp.where(i == j, col, 0.0), axis=0, keepdims=True)


def output_kernel(part_ref, part2_ref, mine_ref, other_ref, out_ref):
    active = lax.axis_index("section") == 0
    g = jnp.where(active, joined(mine_ref[...], other_ref[...]).astype(F32), 0.0)
    out_ref[0] = (g + (part_ref[...].astype(F32) + part2_ref[...].astype(F32))).astype(BF16)


def join_kernel(mine_ref, other_ref, out_ref):
    out_ref[0] = joined(mine_ref[...], other_ref[...])


def shards(section_inputs, cotangent, w_in, w_bc, w_out, decay_rates, resets):
    tokens, width = cotangent.shape
    channels = w_in.shape[2]
    coefs = w_bc.shape[2]
    w_bc = jnp.swapaxes(w_bc, 1, 2)
    states = coefs // 2
    heads = decay_rates.shape[1]
    seq_size = lax.axis_size("seq")
    sections = lax.axis_size("section")
    others = seq_size - 1
    big = 2 * tokens * width * channels
    vec, low = ((tokens, channels), F32), ((tokens, channels), BF16)
    row = ((1, channels), F32)
    few = ((tokens, coefs), F32)
    wide = ((coefs, width), F32)

    up, gmp, coef, a, sa, table, *pay = call(
        functools.partial(start_kernel, seq_size),
        [low, low, ((tokens, coefs), BF16), vec, vec, ((TABLE_ROWS, channels), F32)]
        + [((states, channels + 128), BF16)] * others,
        [
            section_inputs,
            cotangent,
            w_in,
            w_bc,
            w_out,
            decay_rates,
            resets.reshape(1, tokens),
        ],
        space=pltpu.HBM,
        scratch=[
            pltpu.VMEM((tokens, width), BF16),
            pltpu.VMEM((tokens, width), BF16),
            pltpu.VMEM((width, channels), BF16),
            pltpu.VMEM((coefs, width), BF16),
            pltpu.VMEM((channels, width), BF16),
            pltpu.SMEM((1, heads), F32),
            pltpu.VMEM((1, tokens), jnp.int32),
            pltpu.SemaphoreType.DMA((5,)),
            pltpu.SemaphoreType.DMA((OUT_CHUNKS + IN_CHUNKS,)),
        ],
        flops=2 * big,
        bytes_accessed=4 * width * channels,
        name="start",
    )
    recv = [partner(pay[k - 1], "seq", k) for k in ORDERS[0](seq_size)]

    def local(gradient):
        return call(
            local_kernel,
            [vec, few, row],
            [up, gradient, coef],
            flops=big,
            bytes_accessed=4 * tokens * channels,
            name="local",
        )

    def turned(w, after):
        return call(turn_kernel, [((w.shape[2], w.shape[1]), BF16)], [w, after], name="turn")[0]

    w_in_t = turned(w_in, table)
    gu, gcoef, lag = local(gmp)
    state = ((states, channels), F32)
    half = width // 2
    halves = [((tokens, half), F32), ((tokens, half), BF16)]
    keep, send, adj, hpp, weight = call(
        functools.partial(first_kernel, seq_size),
        [*halves, state, state, ((others, channels), F32)],
        [up, gmp, coef, table, sa, w_in_t, w_bc, gu, gcoef, cotangent, *recv],
        flops=big,
        bytes_accessed=2 * width * channels,
        name="first",
    )
    dw, rate = call(
        first_parameter_kernel,
        [wide, row],
        [up, gmp, coef, table, section_inputs, gu, gcoef, lag, hpp, adj],
        flops=big // 4,
        bytes_accessed=4 * tokens * channels,
        name="first_parameters",
    )
    w_out_t = turned(w_out, rate)
    section = lax.axis_index("section")
    kept, kept_dw, kept_rate = None, dw, rate
    for moment in range(1, sections):
        result = (keep + swap(send, "mp").astype(F32)).astype(BF16)
        if kept is None:
            kept = result
        else:
            was_active = section == sections - moment
            kept = jnp.where(was_active, result, kept)
            kept_dw = jnp.where(was_active, dw, kept_dw)
            kept_rate = jnp.where(was_active, rate, kept_rate)
        mine = rotate(result, "section", -1)
        if moment == 1:
            mine, kept_dw, kept_rate, w_out_t = lax.optimization_barrier(
                (mine, kept_dw, kept_rate, w_out_t)
            )
        other = swap(mine, "mp")
        gmp, adjoint = call(
            hop_kernel,
            [low, ((states, channels), BF16)],
            [w_out_t, coef, a, table, mine, other],
            flops=big,
            bytes_accessed=2 * width * channels,
            name="hop",
        )
        recv = [partner(adjoint, "seq", k) for k in ORDERS[1](seq_size)]
        gu, gcoef, lag = local(gmp)
        last = moment == sections - 1
        adj, rows, gcoef, *dw = call(
            functools.partial(parameter_kernel, last, seq_size),
            [state, ((coefs, channels), BF16), ((tokens, coefs), BF16)]
            + ([((coefs, half), F32), ((coefs, half), BF16)] if last else [wide]),
            [up, gmp, table, section_inputs, gcoef, hpp, weight, kept_dw, *recv],
            flops=big // 4,
            bytes_accessed=4 * tokens * channels,
            name="parameters",
        )
        (rate,) = call(
            functools.partial(rate_kernel, last),
            [row],
            [up, gmp, coef, table, gu, lag, hpp, adj, kept_rate],
            flops=big // 8,
            bytes_accessed=4 * tokens * channels,
            name="rates",
        )
        if not last:
            (dw,) = dw
            keep, send = call(
                middle_input_kernel,
                halves,
                [rows, gu, gcoef, coef, sa, w_in_t, w_bc, mine, other],
                flops=big,
                bytes_accessed=2 * width * channels,
                name="middle_input",
            )
    (red,) = call(
        pair_kernel, [((coefs + 8, half), BF16)], [dw[0], swap(dw[1], "mp"), rate], name="pair"
    )
    (part,) = call(
        last_input_kernel,
        [low],
        [rows, gu, gcoef, coef, sa, w_in_t, w_bc, kept],
        flops=big,
        bytes_accessed=2 * width * channels,
        name="last_input",
    )
    part, red = lax.optimization_barrier((part, red))
    (out,) = call(
        output_kernel,
        [((1, tokens, width), BF16)],
        [part, swap(part, "mp"), mine, other],
        name="output",
    )
    pieces = [partner(red, "seq", k) for k in ORDERS[2](seq_size)]
    red, out = lax.optimization_barrier((red, out))
    grad_w, rate = call(
        functools.partial(total_kernel, seq_size),
        [((coefs, half), F32), ((8, half), F32)],
        [red, *pieces],
        name="total",
    )
    (grad_rates,) = call(head_kernel, [((1, heads), F32)], [rate], name="heads")
    (grad_w,) = call(
        join_kernel, [((1, coefs, width), F32)], [grad_w, swap(grad_w, "mp")], name="join"
    )
    return out, jnp.swapaxes(grad_w, 1, 2), grad_rates


def solution(mesh):
    return jax.shard_map(
        shards,
        mesh=mesh,
        in_specs=(
            P("section", ("groups", "seq"), None),
            P(("groups", "seq"), None),
            P("section", None, "mp"),
            P("section", None, None),
            P("section", "mp", None),
            P("section", "mp"),
            P(("groups", "seq")),
        ),
        out_specs=(
            P("section", ("groups", "seq"), None),
            P("section", "groups", None),
            P("section", ("groups", "mp")),
        ),
        check_vma=False,
    )
```

```python
import functools
import math

import jax
import jax.numpy as jnp
from jax import lax
from jax.experimental import pallas as pl
from jax.experimental.pallas import tpu as pltpu
from jax.sharding import PartitionSpec as P

LOG_KEEP = math.log(0.6)
F32 = jnp.float32
BF16 = jnp.bfloat16

NN = (((1,), (0,)), ((), ()))
NT = (((1,), (1,)), ((), ()))
TN = (((0,), (0,)), ((), ()))

RATE, EMID, ATOT, INV, COUNT = 0, 1, 2, 3, 4
TABLE_ROWS = 8
ORDERS = (lambda n: range(n - 1, 0, -1), lambda n: range(1, n), lambda n: range(1, n))
OUT_CHUNKS, IN_CHUNKS = 1, 1


def mm(a, b, dims):
    return lax.dot_general(a, b, dims, preferred_element_type=F32)


def rotate(value, axis, by):
    n = lax.axis_size(axis)
    return lax.ppermute(value, axis, [(i, (i + by) % n) for i in range(n)])


def partner(value, axis, k):
    n = lax.axis_size(axis)
    return lax.ppermute(value, axis, [(i, i ^ k) for i in range(n)])


def swap(value, axis):
    return rotate(value, axis, 1)


def expm1_small(y):
    return y * (1 + y / 2 * (1 + y / 3 * (1 + y / 4 * (1 + y / 5 * (1 + y / 6)))))


def column(tokens):
    return lax.broadcasted_iota(jnp.int32, (tokens, 1), 0).astype(F32)


def tril_mask(tokens):
    t = lax.broadcasted_iota(jnp.int32, (tokens, tokens), 0)
    s = lax.broadcasted_iota(jnp.int32, (tokens, tokens), 1)
    return t, s


def call(kernel, outs, args, *, space=pltpu.VMEM, scratch=(), flops=0, bytes_accessed=0, name=None):
    if space is pltpu.HBM:
        args = [pltpu.with_memory_space_constraint(a, space) for a in args]
    return pl.pallas_call(
        kernel,
        out_shape=[jax.ShapeDtypeStruct(s, d) for s, d in outs],
        in_specs=[pl.BlockSpec(memory_space=space) for _ in args],
        out_specs=[pl.BlockSpec(memory_space=pltpu.VMEM) for _ in outs],
        scratch_shapes=list(scratch),
        compiler_params=pltpu.CompilerParams(vmem_limit_bytes=24 << 20),
        cost_estimate=pl.CostEstimate(
            flops=flops, bytes_accessed=bytes_accessed, transcendentals=0
        ),
        name=name,
    )(*args)


def start_kernel(
    seq_size,
    x_hbm,
    g_hbm,
    w_in_hbm,
    w_bc_hbm,
    w_out_hbm,
    rates_hbm,
    resets_hbm,
    up_ref,
    gmp_ref,
    coef_ref,
    a_ref,
    sa_ref,
    table_ref,
    *refs,
):
    pay_refs = refs[: seq_size - 1]
    x_ref, g_ref, w_in_ref, w_bc_ref, w_out_ref, rates_ref, resets_ref, small_sem, wide_sem = refs[
        seq_size - 1 :
    ]
    tokens = x_hbm.shape[1]
    channels = w_in_hbm.shape[2]
    heads = rates_hbm.shape[1]
    width = channels // heads
    states = w_bc_hbm.shape[1] // 2
    small = [
        pltpu.make_async_copy(src, dst, small_sem.at[i])
        for i, (src, dst) in enumerate(
            [
                (rates_hbm, rates_ref),
                (resets_hbm, resets_ref),
                (g_hbm, g_ref),
                (x_hbm.at[0], x_ref),
                (w_bc_hbm.at[0], w_bc_ref),
            ]
        )
    ]
    rows, cols = channels // OUT_CHUNKS, channels // IN_CHUNKS
    out_parts = [slice(c * rows, (c + 1) * rows) for c in range(OUT_CHUNKS)]
    in_parts = [slice(c * cols, (c + 1) * cols) for c in range(IN_CHUNKS)]
    from_out = [
        pltpu.make_async_copy(w_out_hbm.at[0, p, :], w_out_ref.at[p, :], wide_sem.at[i])
        for i, p in enumerate(out_parts)
    ]
    from_in = [
        pltpu.make_async_copy(w_in_hbm.at[0, :, p], w_in_ref.at[:, p], wide_sem.at[OUT_CHUNKS + i])
        for i, p in enumerate(in_parts)
    ]
    for copy in small[:3] + from_out + small[3:] + from_in:
        copy.start()
    small[0].wait()
    small[1].wait()

    lane_head = lax.broadcasted_iota(jnp.int32, (1, channels), 1) // width
    rate = jnp.zeros((1, channels), F32)
    for k in range(heads):
        rate = jnp.where(lane_head == k, rates_ref[0, k], rate)
    t, s = tril_mask(tokens)
    resets = resets_ref[...].astype(F32)
    count = jnp.sum(jnp.where(s <= t, resets, 0.0), axis=1, keepdims=True)
    log = count * LOG_KEEP - (column(tokens) + 1.0) * rate
    mid = log[tokens // 2 - 1 : tokens // 2, :]
    a = jnp.exp(log - mid)
    growth = expm1_small(2.0 * rate)
    scale = jnp.sqrt(growth / (1.0 + growth))
    emid = jnp.exp(mid)
    atot = a[tokens - 1 : tokens, :]
    a_ref[...] = a
    total = jnp.broadcast_to(count[tokens - 1 : tokens, :], (1, channels))
    table_ref[...] = jnp.concatenate(
        [rate, emid, atot, 1.0 / growth, total, jnp.zeros((TABLE_ROWS - 5, channels), F32)], axis=0
    )

    small[2].wait()
    g = g_ref[...]
    for copy, part in zip(from_out, out_parts):
        copy.wait()
        gmp_ref[:, part] = (mm(g, w_out_ref[part, :], NT) * a[:, part]).astype(BF16)
    small[3].wait()
    small[4].wait()
    x = x_ref[...]
    coef = mm(x, w_bc_ref[...], NT).astype(BF16)
    coef_ref[...] = coef
    adjoint = emid * mm(coef, gmp_ref[...], TN)[states:, :]
    sa = scale / a
    sa_ref[...] = sa
    state = []
    for copy, part in zip(from_in, in_parts):
        copy.wait()
        inner = mm(x, w_in_ref[:, part], NN)
        up = (inner.astype(BF16).astype(F32) * sa[:, part]).astype(BF16)
        up_ref[:, part] = up
        state.append(atot[:, part] * mm(coef, up, TN)[:states, :])
    state = jnp.concatenate(state, axis=1)
    me = lax.axis_index("seq")
    tail = jnp.broadcast_to(count[tokens - 1 : tokens, :], (states, 128)).astype(BF16)
    for k in range(1, seq_size):
        forward = (me ^ k) > me
        pay_refs[k - 1][:, :channels] = jnp.where(forward, state, adjoint).astype(BF16)
        pay_refs[k - 1][:, channels:] = tail


def split(value):
    half = value.shape[1] // 2
    low = lax.axis_index("mp") == 0
    left, right = value[:, :half], value[:, half:]
    return jnp.where(low, left, right), jnp.where(low, right, left)


def joined(mine, other):
    low = lax.axis_index("mp") == 0
    return jnp.concatenate([jnp.where(low, mine, other), jnp.where(low, other, mine)], axis=1)


def turn_kernel(w_ref, after_ref, out_ref):
    out_ref[...] = w_ref[0].T


def coef_grads(gs, b_part, c_part):
    return jnp.concatenate([mm(gs, c_part, TN), mm(gs, b_part, NN)], axis=1)


def local_kernel(up_ref, gmp_ref, coef_ref, *refs):
    hpp_refs, (gu_ref, gcoef_ref, lag_ref) = refs[:-3], refs[-3:]
    tokens = up_ref.shape[0]
    states = coef_ref.shape[1] // 2
    up, gmp = up_ref[...], gmp_ref[...]
    coef = coef_ref[...]
    b_part, c_part = coef[:, :states], coef[:, states:]
    t, s = tril_mask(tokens)
    causal = s <= t
    scores = jnp.where(causal, mm(c_part, b_part, NT), 0.0)
    gu_ref[...] = mm(scores.astype(BF16), gmp, TN)
    lagged = (scores * (t - s).astype(F32)).astype(BF16)
    lag_ref[...] = jnp.sum(gmp.astype(F32) * mm(lagged, up, NN), axis=0, keepdims=True)
    gs = jnp.where(causal, mm(gmp, up, NT), 0.0).astype(BF16)
    gcoef = coef_grads(gs, b_part, c_part)
    for hpp_ref in hpp_refs:
        gcoef = gcoef + mm(gmp, state_rows(hpp_ref[...]), NT)
    gcoef_ref[...] = gcoef


def unpack(seq_size, recv_refs, table_ref, states, tokens):
    channels = table_ref.shape[1]
    rate = table_ref[RATE : RATE + 1, :]
    me = lax.axis_index("seq")
    source = [me ^ k for k in ORDERS[0](seq_size)]
    data = [r[:, :channels].astype(F32) for r in recv_refs]
    gap = [
        r[:1, channels : channels + 1].astype(F32) * LOG_KEEP - tokens * rate for r in recv_refs
    ]
    h_in = jnp.zeros((states, channels), F32)
    adj = jnp.zeros((states, channels), F32)
    weights = []
    for i, src in enumerate(source):
        forward = src < me
        low, high = jnp.minimum(src, me), jnp.maximum(src, me)
        log = jnp.zeros((1, channels), F32)
        for j, other in enumerate(source):
            if j != i:
                between = jnp.logical_and(other > low, other < high)
                log = log + jnp.where(between, gap[j], 0.0)
        weight = jnp.exp(log)
        term = weight * data[i]
        h_in = h_in + jnp.where(forward, term, 0.0)
        adj = adj + jnp.where(forward, 0.0, term)
        weights.append(jnp.where(forward, 0.0, weight))
    return h_in, adj, weights


def state_rows(hpp):
    return jnp.concatenate([jnp.zeros_like(hpp), hpp], axis=0).astype(BF16)


def input_gradient(rows, gu, gcoef, coef, sa_ref, w_in_ref, w_bc_ref):
    grad_inner = (sa_ref[...] * (gu + mm(coef, rows, NN))).astype(BF16)
    return mm(grad_inner, w_in_ref[...], NN) + mm(gcoef, w_bc_ref[0], NN)


def adjoint_rows(adj, table_ref):
    adjp = table_ref[ATOT : ATOT + 1, :] * adj
    return jnp.concatenate([adjp, jnp.zeros_like(adjp)], axis=0).astype(BF16)


def coef_total(rows, h_rows, gcoef_ref, up, gmp):
    return (gcoef_ref[...] + mm(gmp, h_rows, NT) + mm(up, rows, NT)).astype(BF16)


def rate_gradients(adj, hpp, gu_ref, lag_ref, up_ref, gmp_ref, coef_ref, table_ref):
    tokens = up_ref.shape[0]
    coef = coef_ref[...]
    adjp = table_ref[ATOT : ATOT + 1, :] * adj
    v = mm(coef, adjoint_rows(adj, table_ref), NN)
    ch = mm(coef, state_rows(hpp), NN)
    place = column(tokens)
    up_f, gmp_f = up_ref[...].astype(F32), gmp_ref[...].astype(F32)
    lag = (
        lag_ref[...]
        + jnp.sum(gmp_f * ((place + 1.0) * ch), axis=0, keepdims=True)
        + jnp.sum(up_f * ((tokens - 1.0 - place) * v), axis=0, keepdims=True)
        + tokens * jnp.sum(hpp * adjp, axis=0, keepdims=True)
    )
    total = jnp.sum(up_f * (gu_ref[...] + v), axis=0, keepdims=True)
    return total * table_ref[INV : INV + 1, :] - lag


def first_kernel(
    seq_size,
    up_ref,
    gmp_ref,
    coef_ref,
    table_ref,
    sa_ref,
    w_in_ref,
    w_bc_ref,
    gu_ref,
    gcoef_ref,
    g_ref,
    *refs,
):
    recv_refs, (keep_ref, send_ref, adj_ref, hpp_ref, weight_ref) = (
        refs[: seq_size - 1],
        refs[seq_size - 1 :],
    )
    tokens = up_ref.shape[0]
    states = coef_ref.shape[1] // 2
    h_in, adj, weights = unpack(seq_size, recv_refs, table_ref, states, tokens)
    hpp = table_ref[EMID : EMID + 1, :] * h_in
    hpp_ref[...] = hpp
    for k, weight in zip(ORDERS[0](seq_size), weights):
        weight_ref[k - 1 : k, :] = weight
    adj_ref[...] = adj
    rows = adjoint_rows(adj, table_ref)
    gcoef = coef_total(rows, state_rows(hpp), gcoef_ref, up_ref[...], gmp_ref[...])
    back = input_gradient(rows, gu_ref[...], gcoef, coef_ref[...], sa_ref, w_in_ref, w_bc_ref)
    store_split(back, g_ref[...], keep_ref, send_ref)


def store_split(back, g, keep_ref, send_ref):
    keep, send = split(back)
    keep_ref[...] = keep + split(g)[0].astype(F32)
    send_ref[...] = send.astype(BF16)


def gather_adjoint(recv_refs, weight_ref):
    adj = None
    for k, r in zip(ORDERS[1](len(recv_refs) + 1), recv_refs):
        term = weight_ref[k - 1 : k, :] * r[...].astype(F32)
        adj = term if adj is None else adj + term
    return adj


def first_parameter_kernel(
    up_ref,
    gmp_ref,
    coef_ref,
    table_ref,
    x_ref,
    gu_ref,
    gcoef_ref,
    lag_ref,
    hpp_ref,
    adj_ref,
    dw_ref,
    rate_ref,
):
    adj, hpp = adj_ref[...], hpp_ref[...]
    gcoef = coef_total(
        adjoint_rows(adj, table_ref), state_rows(hpp), gcoef_ref, up_ref[...], gmp_ref[...]
    )
    dw_ref[...] = mm(gcoef, x_ref[0], TN)
    rate_ref[...] = rate_gradients(
        adj, hpp, gu_ref, lag_ref, up_ref, gmp_ref, coef_ref, table_ref
    )


def parameter_kernel(
    last,
    seq_size,
    up_ref,
    table_ref,
    x_ref,
    gcoef_in_ref,
    weight_ref,
    kept_ref,
    *refs,
):
    recv_refs, (adj_ref, rows_ref, gcoef_ref, *out_refs) = refs[: seq_size - 1], refs[seq_size - 1 :]
    adj = gather_adjoint(recv_refs, weight_ref)
    adj_ref[...] = adj
    rows = adjoint_rows(adj, table_ref)
    rows_ref[...] = rows
    gcoef = (gcoef_in_ref[...] + mm(up_ref[...], rows, NT)).astype(BF16)
    gcoef_ref[...] = gcoef
    dw = mm(gcoef, x_ref[0], TN)
    if not last:
        out_refs[0][...] = dw
        return
    keep_ref, send_ref = out_refs
    keep_ref[...], send = split(jnp.where(lax.axis_index("section") == 0, dw, kept_ref[...]))
    send_ref[...] = send.astype(BF16)


def rate_kernel(
    last,
    up_ref,
    gmp_ref,
    coef_ref,
    table_ref,
    gu_ref,
    lag_ref,
    hpp_ref,
    adj_ref,
    kept_ref,
    rate_ref,
):
    rate = rate_gradients(
        adj_ref[...], hpp_ref[...], gu_ref, lag_ref, up_ref, gmp_ref, coef_ref, table_ref
    )
    if last:
        rate = jnp.where(lax.axis_index("section") == 0, rate, kept_ref[...])
    rate_ref[...] = rate


def middle_input_kernel(
    rows_ref, gu_ref, gcoef_ref, coef_ref, sa_ref, w_in_ref, w_bc_ref, mine_ref, other_ref, keep_ref, send_ref
):
    back = input_gradient(
        rows_ref[...], gu_ref[...], gcoef_ref[...], coef_ref[...], sa_ref, w_in_ref, w_bc_ref
    )
    store_split(back, joined(mine_ref[...], other_ref[...]), keep_ref, send_ref)


def last_input_kernel(
    rows_ref, gu_ref, gcoef_ref, coef_ref, sa_ref, w_in_ref, w_bc_ref, kept_ref, part_ref
):
    back = input_gradient(
        rows_ref[...], gu_ref[...], gcoef_ref[...], coef_ref[...], sa_ref, w_in_ref, w_bc_ref
    )
    half = kept_ref[...]
    zero = jnp.zeros_like(half)
    low = lax.axis_index("mp") == 0
    done = jnp.concatenate([jnp.where(low, half, zero), jnp.where(low, zero, half)], axis=1)
    part_ref[...] = jnp.where(lax.axis_index("section") == 0, back.astype(BF16), done)


def half_product(g_ref, w_ref, which):
    half = g_ref.shape[1]
    return mm(g_ref[...], w_ref[pl.ds(pl.multiple_of(which * half, half), half), :], NN)


def near_kernel(w_out_ref, mine_ref, near_ref):
    near_ref[...] = half_product(mine_ref, w_out_ref, lax.axis_index("mp"))


def hop_kernel(
    w_out_ref, coef_ref, a_ref, table_ref, near_ref, other_ref, gmp_ref, adjoint_ref
):
    gm = near_ref[...] + half_product(other_ref, w_out_ref, 1 - lax.axis_index("mp"))
    gmp = (a_ref[...] * gm).astype(BF16)
    states = coef_ref.shape[1] // 2
    adjoint = table_ref[EMID : EMID + 1, :] * mm(coef_ref[...], gmp, TN)[states:, :]
    gmp_ref[...] = gmp
    adjoint_ref[...] = adjoint.astype(BF16)


def pair_kernel(keep_ref, other_ref, rate_ref, sum_ref):
    coefs, half = keep_ref.shape
    sum_ref[:coefs, :] = (keep_ref[...] + other_ref[...].astype(F32)).astype(BF16)
    rate = jnp.concatenate([rate_ref[:, :half], rate_ref[:, half:], jnp.zeros((6, half), F32)], axis=0)
    sum_ref[coefs:, :] = rate.astype(BF16)


def total_kernel(seq_size, *refs):
    pieces, (w_ref, rate_ref) = refs[:seq_size], refs[seq_size:]
    ranges = [0, *ORDERS[2](seq_size)]
    terms = [pieces[ranges.index(k)][...].astype(F32) for k in range(seq_size)]
    while len(terms) > 1:
        terms = [x + y for x, y in zip(terms[::2], terms[1::2])]
    total = terms[0]
    coefs = w_ref.shape[0]
    w_ref[...] = total[:coefs, :]
    rate_ref[...] = total[coefs:, :]


def head_kernel(row_ref, rate_ref):
    heads, channels = rate_ref.shape[1], 2 * row_ref.shape[1]
    row = jnp.concatenate([row_ref[:1, :], row_ref[1:2, :]], axis=1)
    lane = lax.broadcasted_iota(jnp.int32, (heads, channels), 1) // (channels // heads)
    head = lax.broadcasted_iota(jnp.int32, (heads, channels), 0)
    col = jnp.sum(jnp.where(lane == head, row, 0.0), axis=1, keepdims=True)
    i = lax.broadcasted_iota(jnp.int32, (heads, heads), 0)
    j = lax.broadcasted_iota(jnp.int32, (heads, heads), 1)
    rate_ref[...] = jnp.sum(jnp.where(i == j, col, 0.0), axis=0, keepdims=True)


def output_kernel(part_ref, part2_ref, mine_ref, other_ref, out_ref):
    active = lax.axis_index("section") == 0
    g = jnp.where(active, joined(mine_ref[...], other_ref[...]).astype(F32), 0.0)
    out_ref[0] = (g + (part_ref[...].astype(F32) + part2_ref[...].astype(F32))).astype(BF16)


def join_kernel(mine_ref, other_ref, out_ref):
    out_ref[0] = joined(mine_ref[...], other_ref[...])


def shards(section_inputs, cotangent, w_in, w_bc, w_out, decay_rates, resets):
    tokens, width = cotangent.shape
    channels = w_in.shape[2]
    coefs = w_bc.shape[2]
    w_bc = jnp.swapaxes(w_bc, 1, 2)
    states = coefs // 2
    heads = decay_rates.shape[1]
    seq_size = lax.axis_size("seq")
    sections = lax.axis_size("section")
    others = seq_size - 1
    big = 2 * tokens * width * channels
    vec, low = ((tokens, channels), F32), ((tokens, channels), BF16)
    row = ((1, channels), F32)
    few = ((tokens, coefs), F32)
    wide = ((coefs, width), F32)

    up, gmp, coef, a, sa, table, *pay = call(
        functools.partial(start_kernel, seq_size),
        [low, low, ((tokens, coefs), BF16), vec, vec, ((TABLE_ROWS, channels), F32)]
        + [((states, channels + 128), BF16)] * others,
        [
            section_inputs,
            cotangent,
            w_in,
            w_bc,
            w_out,
            decay_rates,
            resets.reshape(1, tokens),
        ],
        space=pltpu.HBM,
        scratch=[
            pltpu.VMEM((tokens, width), BF16),
            pltpu.VMEM((tokens, width), BF16),
            pltpu.VMEM((width, channels), BF16),
            pltpu.VMEM((coefs, width), BF16),
            pltpu.VMEM((channels, width), BF16),
            pltpu.SMEM((1, heads), F32),
            pltpu.VMEM((1, tokens), jnp.int32),
            pltpu.SemaphoreType.DMA((5,)),
            pltpu.SemaphoreType.DMA((OUT_CHUNKS + IN_CHUNKS,)),
        ],
        flops=2 * big,
        bytes_accessed=4 * width * channels,
        name="start",
    )
    recv = [partner(pay[k - 1], "seq", k) for k in ORDERS[0](seq_size)]

    def local(gradient, *state_in):
        return call(
            local_kernel,
            [vec, few, row],
            [up, gradient, coef, *state_in],
            flops=big,
            bytes_accessed=4 * tokens * channels,
            name="local",
        )

    def turned(w, after):
        return call(turn_kernel, [((w.shape[2], w.shape[1]), BF16)], [w, after], name="turn")[0]

    w_in_t = turned(w_in, table)
    gu, gcoef, lag = local(gmp)
    state = ((states, channels), F32)
    half = width // 2
    halves = [((tokens, half), F32), ((tokens, half), BF16)]
    keep, send, adj, hpp, weight = call(
        functools.partial(first_kernel, seq_size),
        [*halves, state, state, ((others, channels), F32)],
        [up, gmp, coef, table, sa, w_in_t, w_bc, gu, gcoef, cotangent, *recv],
        flops=big,
        bytes_accessed=2 * width * channels,
        name="first",
    )
    dw, rate = call(
        first_parameter_kernel,
        [wide, row],
        [up, gmp, coef, table, section_inputs, gu, gcoef, lag, hpp, adj],
        flops=big // 4,
        bytes_accessed=4 * tokens * channels,
        name="first_parameters",
    )
    w_out_t = turned(w_out, rate)
    section = lax.axis_index("section")
    kept, kept_dw, kept_rate = None, dw, rate
    for moment in range(1, sections):
        result = (keep + swap(send, "mp").astype(F32)).astype(BF16)
        if kept is None:
            kept = result
        else:
            was_active = section == sections - moment
            kept = jnp.where(was_active, result, kept)
            kept_dw = jnp.where(was_active, dw, kept_dw)
            kept_rate = jnp.where(was_active, rate, kept_rate)
        mine = rotate(result, "section", -1)
        if moment == 1:
            mine, kept_dw, kept_rate, w_out_t = lax.optimization_barrier(
                (mine, kept_dw, kept_rate, w_out_t)
            )
        other = swap(mine, "mp")
        (near,) = call(near_kernel, [vec], [w_out_t, mine], name="near")
        gmp, adjoint = call(
            hop_kernel,
            [low, ((states, channels), BF16)],
            [w_out_t, coef, a, table, near, other],
            flops=big,
            bytes_accessed=2 * width * channels,
            name="hop",
        )
        recv = [partner(adjoint, "seq", k) for k in ORDERS[1](seq_size)]
        gu, gcoef, lag = local(gmp, hpp)
        last = moment == sections - 1
        adj, rows, gcoef, *dw = call(
            functools.partial(parameter_kernel, last, seq_size),
            [state, ((coefs, channels), BF16), ((tokens, coefs), BF16)]
            + ([((coefs, half), F32), ((coefs, half), BF16)] if last else [wide]),
            [up, table, section_inputs, gcoef, weight, kept_dw, *recv],
            flops=big // 4,
            bytes_accessed=4 * tokens * channels,
            name="parameters",
        )
        (rate,) = call(
            functools.partial(rate_kernel, last),
            [row],
            [up, gmp, coef, table, gu, lag, hpp, adj, kept_rate],
            flops=big // 8,
            bytes_accessed=4 * tokens * channels,
            name="rates",
        )
        if not last:
            (dw,) = dw
            keep, send = call(
                middle_input_kernel,
                halves,
                [rows, gu, gcoef, coef, sa, w_in_t, w_bc, mine, other],
                flops=big,
                bytes_accessed=2 * width * channels,
                name="middle_input",
            )
    (red,) = call(
        pair_kernel, [((coefs + 8, half), BF16)], [dw[0], swap(dw[1], "mp"), rate], name="pair"
    )
    (part,) = call(
        last_input_kernel,
        [low],
        [rows, gu, gcoef, coef, sa, w_in_t, w_bc, kept],
        flops=big,
        bytes_accessed=2 * width * channels,
        name="last_input",
    )
    part, red = lax.optimization_barrier((part, red))
    (out,) = call(
        output_kernel,
        [((1, tokens, width), BF16)],
        [part, swap(part, "mp"), mine, other],
        name="output",
    )
    pieces = [partner(red, "seq", k) for k in ORDERS[2](seq_size)]
    red, out = lax.optimization_barrier((red, out))
    grad_w, rate = call(
        functools.partial(total_kernel, seq_size),
        [((coefs, half), F32), ((8, half), F32)],
        [red, *pieces],
        name="total",
    )
    (grad_rates,) = call(head_kernel, [((1, heads), F32)], [rate], name="heads")
    (grad_w,) = call(
        join_kernel, [((1, coefs, width), F32)], [grad_w, swap(grad_w, "mp")], name="join"
    )
    return out, jnp.swapaxes(grad_w, 1, 2), grad_rates


def solution(mesh):
    return jax.shard_map(
        shards,
        mesh=mesh,
        in_specs=(
            P("section", ("groups", "seq"), None),
            P(("groups", "seq"), None),
            P("section", None, "mp"),
            P("section", None, None),
            P("section", "mp", None),
            P("section", "mp"),
            P(("groups", "seq")),
        ),
        out_specs=(
            P("section", ("groups", "seq"), None),
            P("section", "groups", None),
            P("section", ("groups", "mp")),
        ),
        check_vma=False,
    )
```

```python
import functools
import math

import jax
import jax.numpy as jnp
from jax import lax
from jax.experimental import pallas as pl
from jax.experimental.pallas import tpu as pltpu
from jax.sharding import PartitionSpec as P

LOG_KEEP = math.log(0.6)
F32 = jnp.float32
BF16 = jnp.bfloat16

NN = (((1,), (0,)), ((), ()))
NT = (((1,), (1,)), ((), ()))
TN = (((0,), (0,)), ((), ()))

RATE, EMID, ATOT, INV, COUNT = 0, 1, 2, 3, 4
TABLE_ROWS = 8
ORDERS = (
    lambda n: range(n - 1, 0, -1),
    lambda n: range(1, n),
    lambda n: (2, 1, *range(3, n)),
)
OUT_CHUNKS, IN_CHUNKS = 1, 1


def mm(a, b, dims):
    return lax.dot_general(a, b, dims, preferred_element_type=F32)


def rotate(value, axis, by):
    n = lax.axis_size(axis)
    return lax.ppermute(value, axis, [(i, (i + by) % n) for i in range(n)])


def partner(value, axis, k):
    n = lax.axis_size(axis)
    return lax.ppermute(value, axis, [(i, i ^ k) for i in range(n)])


def swap(value, axis):
    return rotate(value, axis, 1)


def expm1_small(y):
    return y * (1 + y / 2 * (1 + y / 3 * (1 + y / 4 * (1 + y / 5 * (1 + y / 6)))))


def column(tokens):
    return lax.broadcasted_iota(jnp.int32, (tokens, 1), 0).astype(F32)


def tril_mask(tokens):
    t = lax.broadcasted_iota(jnp.int32, (tokens, tokens), 0)
    s = lax.broadcasted_iota(jnp.int32, (tokens, tokens), 1)
    return t, s


def call(kernel, outs, args, *, space=pltpu.VMEM, scratch=(), flops=0, bytes_accessed=0, name=None):
    if space is pltpu.HBM:
        args = [pltpu.with_memory_space_constraint(a, space) for a in args]
    return pl.pallas_call(
        kernel,
        out_shape=[jax.ShapeDtypeStruct(s, d) for s, d in outs],
        in_specs=[pl.BlockSpec(memory_space=space) for _ in args],
        out_specs=[pl.BlockSpec(memory_space=pltpu.VMEM) for _ in outs],
        scratch_shapes=list(scratch),
        compiler_params=pltpu.CompilerParams(vmem_limit_bytes=24 << 20),
        cost_estimate=pl.CostEstimate(
            flops=flops, bytes_accessed=bytes_accessed, transcendentals=0
        ),
        name=name,
    )(*args)


def start_kernel(
    seq_size,
    x_hbm,
    g_hbm,
    w_in_hbm,
    w_bc_hbm,
    w_out_hbm,
    rates_hbm,
    resets_hbm,
    up_ref,
    gmp_ref,
    coef_ref,
    a_ref,
    sa_ref,
    table_ref,
    *refs,
):
    pay_refs = refs[: seq_size - 1]
    x_ref, g_ref, w_in_ref, w_bc_ref, w_out_ref, rates_ref, resets_ref, small_sem, wide_sem = refs[
        seq_size - 1 :
    ]
    tokens = x_hbm.shape[1]
    channels = w_in_hbm.shape[2]
    heads = rates_hbm.shape[1]
    width = channels // heads
    states = w_bc_hbm.shape[1] // 2
    small = [
        pltpu.make_async_copy(src, dst, small_sem.at[i])
        for i, (src, dst) in enumerate(
            [
                (rates_hbm, rates_ref),
                (resets_hbm, resets_ref),
                (g_hbm, g_ref),
                (x_hbm.at[0], x_ref),
                (w_bc_hbm.at[0], w_bc_ref),
            ]
        )
    ]
    rows, cols = channels // OUT_CHUNKS, channels // IN_CHUNKS
    out_parts = [slice(c * rows, (c + 1) * rows) for c in range(OUT_CHUNKS)]
    in_parts = [slice(c * cols, (c + 1) * cols) for c in range(IN_CHUNKS)]
    from_out = [
        pltpu.make_async_copy(w_out_hbm.at[0, p, :], w_out_ref.at[p, :], wide_sem.at[i])
        for i, p in enumerate(out_parts)
    ]
    from_in = [
        pltpu.make_async_copy(w_in_hbm.at[0, :, p], w_in_ref.at[:, p], wide_sem.at[OUT_CHUNKS + i])
        for i, p in enumerate(in_parts)
    ]
    for copy in small[:3] + from_out + small[3:] + from_in:
        copy.start()
    small[0].wait()
    small[1].wait()

    lane_head = lax.broadcasted_iota(jnp.int32, (1, channels), 1) // width
    rate = jnp.zeros((1, channels), F32)
    for k in range(heads):
        rate = jnp.where(lane_head == k, rates_ref[0, k], rate)
    t, s = tril_mask(tokens)
    resets = resets_ref[...].astype(F32)
    count = jnp.sum(jnp.where(s <= t, resets, 0.0), axis=1, keepdims=True)
    log = count * LOG_KEEP - (column(tokens) + 1.0) * rate
    mid = log[tokens // 2 - 1 : tokens // 2, :]
    a = jnp.exp(log - mid)
    growth = expm1_small(2.0 * rate)
    scale = jnp.sqrt(growth / (1.0 + growth))
    emid = jnp.exp(mid)
    atot = a[tokens - 1 : tokens, :]
    a_ref[...] = a
    total = jnp.broadcast_to(count[tokens - 1 : tokens, :], (1, channels))
    table_ref[...] = jnp.concatenate(
        [rate, emid, atot, 1.0 / growth, total, jnp.zeros((TABLE_ROWS - 5, channels), F32)], axis=0
    )

    small[2].wait()
    g = g_ref[...]
    for copy, part in zip(from_out, out_parts):
        copy.wait()
        gmp_ref[:, part] = (mm(g, w_out_ref[part, :], NT) * a[:, part]).astype(BF16)
    small[3].wait()
    small[4].wait()
    x = x_ref[...]
    coef = mm(x, w_bc_ref[...], NT).astype(BF16)
    coef_ref[...] = coef
    adjoint = emid * mm(coef, gmp_ref[...], TN)[states:, :]
    sa = scale / a
    sa_ref[...] = sa
    state = []
    for copy, part in zip(from_in, in_parts):
        copy.wait()
        inner = mm(x, w_in_ref[:, part], NN)
        up = (inner.astype(BF16).astype(F32) * sa[:, part]).astype(BF16)
        up_ref[:, part] = up
        state.append(atot[:, part] * mm(coef, up, TN)[:states, :])
    state = jnp.concatenate(state, axis=1)
    me = lax.axis_index("seq")
    tail = jnp.broadcast_to(count[tokens - 1 : tokens, :], (states, 128)).astype(BF16)
    for k in range(1, seq_size):
        forward = (me ^ k) > me
        pay_refs[k - 1][:, :channels] = jnp.where(forward, state, adjoint).astype(BF16)
        pay_refs[k - 1][:, channels:] = tail


def split(value):
    half = value.shape[1] // 2
    low = lax.axis_index("mp") == 0
    left, right = value[:, :half], value[:, half:]
    return jnp.where(low, left, right), jnp.where(low, right, left)


def joined(mine, other):
    low = lax.axis_index("mp") == 0
    return jnp.concatenate([jnp.where(low, mine, other), jnp.where(low, other, mine)], axis=1)


def turn_kernel(w_ref, after_ref, out_ref):
    out_ref[...] = w_ref[0].T


def coef_grads(gs, b_part, c_part):
    return jnp.concatenate([mm(gs, c_part, TN), mm(gs, b_part, NN)], axis=1)


def local_kernel(up_ref, gmp_ref, coef_ref, *refs):
    hpp_refs, (gu_ref, gcoef_ref, lag_ref) = refs[:-3], refs[-3:]
    tokens = up_ref.shape[0]
    states = coef_ref.shape[1] // 2
    up, gmp = up_ref[...], gmp_ref[...]
    coef = coef_ref[...]
    b_part, c_part = coef[:, :states], coef[:, states:]
    t, s = tril_mask(tokens)
    causal = s <= t
    scores = jnp.where(causal, mm(c_part, b_part, NT), 0.0)
    gu_ref[...] = mm(scores.astype(BF16), gmp, TN)
    lagged = (scores * (t - s).astype(F32)).astype(BF16)
    lag_ref[...] = jnp.sum(gmp.astype(F32) * mm(lagged, up, NN), axis=0, keepdims=True)
    gs = jnp.where(causal, mm(gmp, up, NT), 0.0).astype(BF16)
    gcoef = coef_grads(gs, b_part, c_part)
    for hpp_ref in hpp_refs:
        gcoef = gcoef + mm(gmp, state_rows(hpp_ref[...]), NT)
    gcoef_ref[...] = gcoef


def unpack(seq_size, recv_refs, table_ref, states, tokens):
    channels = table_ref.shape[1]
    rate = table_ref[RATE : RATE + 1, :]
    me = lax.axis_index("seq")
    source = [me ^ k for k in ORDERS[0](seq_size)]
    data = [r[:, :channels].astype(F32) for r in recv_refs]
    gap = [
        r[:1, channels : channels + 1].astype(F32) * LOG_KEEP - tokens * rate for r in recv_refs
    ]
    h_in = jnp.zeros((states, channels), F32)
    adj = jnp.zeros((states, channels), F32)
    weights = []
    for i, src in enumerate(source):
        forward = src < me
        low, high = jnp.minimum(src, me), jnp.maximum(src, me)
        log = jnp.zeros((1, channels), F32)
        for j, other in enumerate(source):
            if j != i:
                between = jnp.logical_and(other > low, other < high)
                log = log + jnp.where(between, gap[j], 0.0)
        weight = jnp.exp(log)
        term = weight * data[i]
        h_in = h_in + jnp.where(forward, term, 0.0)
        adj = adj + jnp.where(forward, 0.0, term)
        weights.append(jnp.where(forward, 0.0, weight))
    return h_in, adj, weights


def state_rows(hpp):
    return jnp.concatenate([jnp.zeros_like(hpp), hpp], axis=0).astype(BF16)


def input_gradient(rows, gu, gcoef, coef, sa_ref, w_in_ref, w_bc_ref):
    grad_inner = (sa_ref[...] * (gu + mm(coef, rows, NN))).astype(BF16)
    return mm(grad_inner, w_in_ref[...], NN) + mm(gcoef, w_bc_ref[0], NN)


def adjoint_rows(adj, table_ref):
    adjp = table_ref[ATOT : ATOT + 1, :] * adj
    return jnp.concatenate([adjp, jnp.zeros_like(adjp)], axis=0).astype(BF16)


def coef_total(rows, h_rows, gcoef_ref, up, gmp):
    return (gcoef_ref[...] + mm(gmp, h_rows, NT) + mm(up, rows, NT)).astype(BF16)


def rate_gradients(adj, hpp, gu_ref, lag_ref, up_ref, gmp_ref, coef_ref, table_ref):
    tokens = up_ref.shape[0]
    coef = coef_ref[...]
    adjp = table_ref[ATOT : ATOT + 1, :] * adj
    v = mm(coef, adjoint_rows(adj, table_ref), NN)
    ch = mm(coef, state_rows(hpp), NN)
    place = column(tokens)
    up_f, gmp_f = up_ref[...].astype(F32), gmp_ref[...].astype(F32)
    lag = (
        lag_ref[...]
        + jnp.sum(gmp_f * ((place + 1.0) * ch), axis=0, keepdims=True)
        + jnp.sum(up_f * ((tokens - 1.0 - place) * v), axis=0, keepdims=True)
        + tokens * jnp.sum(hpp * adjp, axis=0, keepdims=True)
    )
    total = jnp.sum(up_f * (gu_ref[...] + v), axis=0, keepdims=True)
    return total * table_ref[INV : INV + 1, :] - lag


def first_kernel(
    seq_size,
    up_ref,
    gmp_ref,
    coef_ref,
    table_ref,
    sa_ref,
    w_in_ref,
    w_bc_ref,
    gu_ref,
    gcoef_ref,
    g_ref,
    *refs,
):
    recv_refs, (keep_ref, send_ref, adj_ref, hpp_ref, weight_ref) = (
        refs[: seq_size - 1],
        refs[seq_size - 1 :],
    )
    tokens = up_ref.shape[0]
    states = coef_ref.shape[1] // 2
    h_in, adj, weights = unpack(seq_size, recv_refs, table_ref, states, tokens)
    hpp = table_ref[EMID : EMID + 1, :] * h_in
    hpp_ref[...] = hpp
    for k, weight in zip(ORDERS[0](seq_size), weights):
        weight_ref[k - 1 : k, :] = weight
    adj_ref[...] = adj
    rows = adjoint_rows(adj, table_ref)
    gcoef = coef_total(rows, state_rows(hpp), gcoef_ref, up_ref[...], gmp_ref[...])
    back = input_gradient(rows, gu_ref[...], gcoef, coef_ref[...], sa_ref, w_in_ref, w_bc_ref)
    store_split(back, g_ref[...], keep_ref, send_ref)


def store_split(back, g, keep_ref, send_ref):
    keep, send = split(back)
    keep_ref[...] = keep + split(g)[0].astype(F32)
    send_ref[...] = send.astype(BF16)


def gather_adjoint(recv_refs, weight_ref):
    adj = None
    for k, r in zip(ORDERS[1](len(recv_refs) + 1), recv_refs):
        term = weight_ref[k - 1 : k, :] * r[...].astype(F32)
        adj = term if adj is None else adj + term
    return adj


def first_parameter_kernel(
    up_ref,
    gmp_ref,
    coef_ref,
    table_ref,
    x_ref,
    gu_ref,
    gcoef_ref,
    lag_ref,
    hpp_ref,
    adj_ref,
    dw_ref,
    rate_ref,
):
    adj, hpp = adj_ref[...], hpp_ref[...]
    gcoef = coef_total(
        adjoint_rows(adj, table_ref), state_rows(hpp), gcoef_ref, up_ref[...], gmp_ref[...]
    )
    dw_ref[...] = mm(gcoef, x_ref[0], TN)
    rate_ref[...] = rate_gradients(
        adj, hpp, gu_ref, lag_ref, up_ref, gmp_ref, coef_ref, table_ref
    )


def parameter_kernel(
    last,
    seq_size,
    up_ref,
    table_ref,
    x_ref,
    gcoef_in_ref,
    weight_ref,
    kept_ref,
    *refs,
):
    recv_refs, (adj_ref, rows_ref, gcoef_ref, *out_refs) = refs[: seq_size - 1], refs[seq_size - 1 :]
    adj = gather_adjoint(recv_refs, weight_ref)
    adj_ref[...] = adj
    rows = adjoint_rows(adj, table_ref)
    rows_ref[...] = rows
    gcoef = (gcoef_in_ref[...] + mm(up_ref[...], rows, NT)).astype(BF16)
    gcoef_ref[...] = gcoef
    dw = mm(gcoef, x_ref[0], TN)
    if not last:
        out_refs[0][...] = dw
        return
    keep_ref, send_ref = out_refs
    keep_ref[...], send = split(jnp.where(lax.axis_index("section") == 0, dw, kept_ref[...]))
    send_ref[...] = send.astype(BF16)


def rate_kernel(
    last,
    up_ref,
    gmp_ref,
    coef_ref,
    table_ref,
    gu_ref,
    lag_ref,
    hpp_ref,
    adj_ref,
    kept_ref,
    rate_ref,
):
    rate = rate_gradients(
        adj_ref[...], hpp_ref[...], gu_ref, lag_ref, up_ref, gmp_ref, coef_ref, table_ref
    )
    if last:
        rate = jnp.where(lax.axis_index("section") == 0, rate, kept_ref[...])
    rate_ref[...] = rate


def middle_input_kernel(
    rows_ref, gu_ref, gcoef_ref, coef_ref, sa_ref, w_in_ref, w_bc_ref, mine_ref, other_ref, keep_ref, send_ref
):
    back = input_gradient(
        rows_ref[...], gu_ref[...], gcoef_ref[...], coef_ref[...], sa_ref, w_in_ref, w_bc_ref
    )
    store_split(back, joined(mine_ref[...], other_ref[...]), keep_ref, send_ref)


def last_input_kernel(
    rows_ref, gu_ref, gcoef_ref, coef_ref, sa_ref, w_in_ref, w_bc_ref, kept_ref, part_ref
):
    back = input_gradient(
        rows_ref[...], gu_ref[...], gcoef_ref[...], coef_ref[...], sa_ref, w_in_ref, w_bc_ref
    )
    half = kept_ref[...]
    zero = jnp.zeros_like(half)
    low = lax.axis_index("mp") == 0
    done = jnp.concatenate([jnp.where(low, half, zero), jnp.where(low, zero, half)], axis=1)
    part_ref[...] = jnp.where(lax.axis_index("section") == 0, back.astype(BF16), done)


def half_product(g_ref, w_ref, which):
    half = g_ref.shape[1]
    return mm(g_ref[...], w_ref[pl.ds(pl.multiple_of(which * half, half), half), :], NN)


def near_kernel(w_out_ref, mine_ref, near_ref):
    near_ref[...] = half_product(mine_ref, w_out_ref, lax.axis_index("mp"))


def hop_kernel(
    w_out_ref, coef_ref, a_ref, table_ref, near_ref, other_ref, gmp_ref, adjoint_ref
):
    gm = near_ref[...] + half_product(other_ref, w_out_ref, 1 - lax.axis_index("mp"))
    gmp = (a_ref[...] * gm).astype(BF16)
    states = coef_ref.shape[1] // 2
    adjoint = table_ref[EMID : EMID + 1, :] * mm(coef_ref[...], gmp, TN)[states:, :]
    gmp_ref[...] = gmp
    adjoint_ref[...] = adjoint.astype(BF16)


def pair_kernel(keep_ref, other_ref, rate_ref, sum_ref):
    coefs, half = keep_ref.shape
    sum_ref[:coefs, :] = (keep_ref[...] + other_ref[...].astype(F32)).astype(BF16)
    rate = jnp.concatenate([rate_ref[:, :half], rate_ref[:, half:], jnp.zeros((6, half), F32)], axis=0)
    sum_ref[coefs:, :] = rate.astype(BF16)


def total_kernel(seq_size, *refs):
    pieces, (w_ref, rate_ref) = refs[:seq_size], refs[seq_size:]
    ranges = [0, *ORDERS[2](seq_size)]
    terms = [pieces[ranges.index(k)][...].astype(F32) for k in range(seq_size)]
    while len(terms) > 1:
        terms = [x + y for x, y in zip(terms[::2], terms[1::2])]
    total = terms[0]
    coefs = w_ref.shape[0]
    w_ref[...] = total[:coefs, :]
    rate_ref[...] = total[coefs:, :]


def head_kernel(row_ref, rate_ref):
    heads, channels = rate_ref.shape[1], 2 * row_ref.shape[1]
    row = jnp.concatenate([row_ref[:1, :], row_ref[1:2, :]], axis=1)
    lane = lax.broadcasted_iota(jnp.int32, (heads, channels), 1) // (channels // heads)
    head = lax.broadcasted_iota(jnp.int32, (heads, channels), 0)
    col = jnp.sum(jnp.where(lane == head, row, 0.0), axis=1, keepdims=True)
    i = lax.broadcasted_iota(jnp.int32, (heads, heads), 0)
    j = lax.broadcasted_iota(jnp.int32, (heads, heads), 1)
    rate_ref[...] = jnp.sum(jnp.where(i == j, col, 0.0), axis=0, keepdims=True)


def output_kernel(part_ref, part2_ref, mine_ref, other_ref, out_ref):
    active = lax.axis_index("section") == 0
    g = jnp.where(active, joined(mine_ref[...], other_ref[...]).astype(F32), 0.0)
    out_ref[0] = (g + (part_ref[...].astype(F32) + part2_ref[...].astype(F32))).astype(BF16)


def join_kernel(mine_ref, other_ref, out_ref):
    out_ref[0] = joined(mine_ref[...], other_ref[...])


def shards(section_inputs, cotangent, w_in, w_bc, w_out, decay_rates, resets):
    tokens, width = cotangent.shape
    channels = w_in.shape[2]
    coefs = w_bc.shape[2]
    w_bc = jnp.swapaxes(w_bc, 1, 2)
    states = coefs // 2
    heads = decay_rates.shape[1]
    seq_size = lax.axis_size("seq")
    sections = lax.axis_size("section")
    others = seq_size - 1
    big = 2 * tokens * width * channels
    vec, low = ((tokens, channels), F32), ((tokens, channels), BF16)
    row = ((1, channels), F32)
    few = ((tokens, coefs), F32)
    wide = ((coefs, width), F32)

    up, gmp, coef, a, sa, table, *pay = call(
        functools.partial(start_kernel, seq_size),
        [low, low, ((tokens, coefs), BF16), vec, vec, ((TABLE_ROWS, channels), F32)]
        + [((states, channels + 128), BF16)] * others,
        [
            section_inputs,
            cotangent,
            w_in,
            w_bc,
            w_out,
            decay_rates,
            resets.reshape(1, tokens),
        ],
        space=pltpu.HBM,
        scratch=[
            pltpu.VMEM((tokens, width), BF16),
            pltpu.VMEM((tokens, width), BF16),
            pltpu.VMEM((width, channels), BF16),
            pltpu.VMEM((coefs, width), BF16),
            pltpu.VMEM((channels, width), BF16),
            pltpu.SMEM((1, heads), F32),
            pltpu.VMEM((1, tokens), jnp.int32),
            pltpu.SemaphoreType.DMA((5,)),
            pltpu.SemaphoreType.DMA((OUT_CHUNKS + IN_CHUNKS,)),
        ],
        flops=2 * big,
        bytes_accessed=4 * width * channels,
        name="start",
    )
    recv = [partner(pay[k - 1], "seq", k) for k in ORDERS[0](seq_size)]

    def local(gradient, *state_in):
        return call(
            local_kernel,
            [vec, few, row],
            [up, gradient, coef, *state_in],
            flops=big,
            bytes_accessed=4 * tokens * channels,
            name="local",
        )

    def turned(w, after):
        return call(turn_kernel, [((w.shape[2], w.shape[1]), BF16)], [w, after], name="turn")[0]

    w_in_t = turned(w_in, table)
    gu, gcoef, lag = local(gmp)
    state = ((states, channels), F32)
    half = width // 2
    halves = [((tokens, half), F32), ((tokens, half), BF16)]
    keep, send, adj, hpp, weight = call(
        functools.partial(first_kernel, seq_size),
        [*halves, state, state, ((others, channels), F32)],
        [up, gmp, coef, table, sa, w_in_t, w_bc, gu, gcoef, cotangent, *recv],
        flops=big,
        bytes_accessed=2 * width * channels,
        name="first",
    )
    dw, rate = call(
        first_parameter_kernel,
        [wide, row],
        [up, gmp, coef, table, section_inputs, gu, gcoef, lag, hpp, adj],
        flops=big // 4,
        bytes_accessed=4 * tokens * channels,
        name="first_parameters",
    )
    w_out_t = turned(w_out, rate)
    section = lax.axis_index("section")
    kept, kept_dw, kept_rate = None, dw, rate
    for moment in range(1, sections):
        result = (keep + swap(send, "mp").astype(F32)).astype(BF16)
        if kept is None:
            kept = result
        else:
            was_active = section == sections - moment
            kept = jnp.where(was_active, result, kept)
            kept_dw = jnp.where(was_active, dw, kept_dw)
            kept_rate = jnp.where(was_active, rate, kept_rate)
        mine = rotate(result, "section", -1)
        if moment == 1:
            mine, kept_dw, kept_rate, w_out_t = lax.optimization_barrier(
                (mine, kept_dw, kept_rate, w_out_t)
            )
        other = swap(mine, "mp")
        (near,) = call(near_kernel, [vec], [w_out_t, mine], name="near")
        gmp, adjoint = call(
            hop_kernel,
            [low, ((states, channels), BF16)],
            [w_out_t, coef, a, table, near, other],
            flops=big,
            bytes_accessed=2 * width * channels,
            name="hop",
        )
        recv = [partner(adjoint, "seq", k) for k in ORDERS[1](seq_size)]
        gu, gcoef, lag = local(gmp, hpp)
        last = moment == sections - 1
        adj, rows, gcoef, *dw = call(
            functools.partial(parameter_kernel, last, seq_size),
            [state, ((coefs, channels), BF16), ((tokens, coefs), BF16)]
            + ([((coefs, half), F32), ((coefs, half), BF16)] if last else [wide]),
            [up, table, section_inputs, gcoef, weight, kept_dw, *recv],
            flops=big // 4,
            bytes_accessed=4 * tokens * channels,
            name="parameters",
        )
        (rate,) = call(
            functools.partial(rate_kernel, last),
            [row],
            [up, gmp, coef, table, gu, lag, hpp, adj, kept_rate],
            flops=big // 8,
            bytes_accessed=4 * tokens * channels,
            name="rates",
        )
        if not last:
            (dw,) = dw
            keep, send = call(
                middle_input_kernel,
                halves,
                [rows, gu, gcoef, coef, sa, w_in_t, w_bc, mine, other],
                flops=big,
                bytes_accessed=2 * width * channels,
                name="middle_input",
            )
    (red,) = call(
        pair_kernel, [((coefs + 8, half), BF16)], [dw[0], swap(dw[1], "mp"), rate], name="pair"
    )
    (part,) = call(
        last_input_kernel,
        [low],
        [rows, gu, gcoef, coef, sa, w_in_t, w_bc, kept],
        flops=big,
        bytes_accessed=2 * width * channels,
        name="last_input",
    )
    part, red = lax.optimization_barrier((part, red))
    (out,) = call(
        output_kernel,
        [((1, tokens, width), BF16)],
        [part, swap(part, "mp"), mine, other],
        name="output",
    )
    pieces = [partner(red, "seq", k) for k in ORDERS[2](seq_size)]
    red, out = lax.optimization_barrier((red, out))
    grad_w, rate = call(
        functools.partial(total_kernel, seq_size),
        [((coefs, half), F32), ((8, half), F32)],
        [red, *pieces],
        name="total",
    )
    (grad_rates,) = call(head_kernel, [((1, heads), F32)], [rate], name="heads")
    (grad_w,) = call(
        join_kernel, [((1, coefs, width), F32)], [grad_w, swap(grad_w, "mp")], name="join"
    )
    return out, jnp.swapaxes(grad_w, 1, 2), grad_rates


def solution(mesh):
    return jax.shard_map(
        shards,
        mesh=mesh,
        in_specs=(
            P("section", ("groups", "seq"), None),
            P(("groups", "seq"), None),
            P("section", None, "mp"),
            P("section", None, None),
            P("section", "mp", None),
            P("section", "mp"),
            P(("groups", "seq")),
        ),
        out_specs=(
            P("section", ("groups", "seq"), None),
            P("section", "groups", None),
            P("section", ("groups", "mp")),
        ),
        check_vma=False,
    )
```
